32 devices in a mesh: dp: 8 (over y, x, core), seq: 4 (over z).
Axes of the slice: x: 2, y: 2, z: 4, core: 2. Of those that a mesh axis runs over, the one named last changes fastest.
Arguments:
- inputs: bfloat16 [8, 1024, 768], P('dp', 'seq'), may hold values from -6 to 6
- block_ids: int32 [8, 4], P('dp'), may hold values from 0 to 1, never falling along the last dimension, each value on 1 to 3 neighbouring positions
- query_weight: bfloat16 [768, 768], P('dp'), may hold values from -0.3125 to 0.3125
- query_bias: bfloat16 [768], P('dp'), may hold values from -3 to 3
- key_weight: bfloat16 [768, 768], P('dp'), may hold values from -0.3125 to 0.3125
- value_weight: bfloat16 [768, 768], P('dp'), may hold values from -0.21875 to 0.21875
- value_bias: bfloat16 [768], P('dp'), may hold values from -3 to 3
- output_weight: bfloat16 [768, 768], P('dp'), may hold values from -1.25 to 1.25
- output_bias: bfloat16 [768], P('dp'), may hold values from -3 to 3
- attention_gain: bfloat16 [768], P('dp'), may hold values from 0.5 to 1.5
- attention_shift: bfloat16 [768], P('dp'), may hold values from -2 to 2
- expand_weight: bfloat16 [768, 3072], P('dp'), may hold values from -0.21875 to 0.21875
- expand_bias: bfloat16 [3072], P('dp'), may hold values from -3 to 3
- reduce_weight: bfloat16 [3072, 768], P('dp'), may hold values from -0.109375 to 0.109375
- reduce_bias: bfloat16 [768], P('dp'), may hold values from -3 to 3
- final_gain: bfloat16 [768], P('dp'), may hold values from 0.5 to 1.5
- final_shift: bfloat16 [768], P('dp'), may hold values from -2 to 2
- cotangent: bfloat16 [8, 1024, 768], P('dp', 'seq'), may hold values from -6 to 6
Outputs:
- output: bfloat16 [8, 1024, 768], P('dp', 'seq')
- input_gradient: float32 [8, 1024, 768], P('dp', 'seq')
- query_matrix: float32 [768, 768], P('dp')
- query_vector: float32 [768], P('dp')
- key_matrix: float32 [768, 768], P('dp')
- value_matrix: float32 [768, 768], P('dp')
- value_vector: float32 [768], P('dp')
- output_matrix: float32 [768, 768], P('dp')
- output_vector: float32 [768], P('dp')
- first_scale: float32 [768], P('dp')
- first_offset: float32 [768], P('dp')
- expand_matrix: float32 [768, 3072], P('dp')
- expand_vector: float32 [3072], P('dp')
- reduce_matrix: float32 [3072, 768], P('dp')
- reduce_vector: float32 [768], P('dp')
- last_scale: float32 [768], P('dp')
- last_offset: float32 [768], P('dp')
The draws below stay inside these ranges and needn't reach their ends.
Inputs may be any that keep to these rules, and one draw needn't show every extreme that they name: block_ids[s, b] is the document of the b-th block of sequence s; two documents in every sequence, each covering 1 to 3 neighbouring blocks (4 in all); numbers never fall along a sequence.
All inputs are finite; a program needn't handle non-finite values.
Results may differ from the reference program's by a relative error of at most 0.018.
Values may be sent and summed in bfloat16 or wider, within the bound.
A program may use at most 128 MiB of HBM per device.

```python
import math
import jax
import jax.numpy as jnp
import numpy as np
from jax import lax

D = 768
HEADS = 12
HD = 64
FF = 3072
BLK = 256
LEN = 1024
NBLK = 4
SEQS = 8


def block_levels(stream_key, shape, split, smallest, largest):
    factor_of = 1.0
    for position, parts in split:
        draws = jax.random.uniform(jax.random.fold_in(jax.random.fold_in(stream_key, 6), position), (parts,), jnp.float32, smallest / len(split), largest / len(split))
        factor_of = factor_of * jnp.repeat(jnp.exp(draws), shape[position] // parts).reshape((-1,) + (1,) * (len(shape) - 1 - position))
    return factor_of


def length_profile(number_of, total, bound, skew):
    weights = [(1 << 20) // math.isqrt(standing ** skew) + 1 for standing in range(2, number_of + 1)]
    surplus, given = total - bound - (number_of - 1), [1] * (number_of - 1)
    while surplus > 0:
        candidates = [i for i in range(number_of - 1) if given[i] < bound]
        mass, budget = sum([weights[i] for i in candidates]), surplus
        for i in candidates:
            addition = min(bound - given[i], max(1, budget * weights[i] // mass), surplus)
            given[i] = given[i] + addition
            surplus = surplus - addition
    return np.array([bound] + given)


def uneven(stream_key, number_of, total, most, skew):
    if number_of == 2:
        one = jax.random.randint(stream_key, (), max(1, total - most), min(most, total - 1) + 1)
        return jnp.stack([one, total - one])
    lengths = jnp.asarray(length_profile(number_of, total, most, skew), jnp.int32)
    pairs = (number_of - 1) // 2
    source_of, receiver = lengths[1:1 + 2 * pairs:2], lengths[2:2 + 2 * pairs:2]
    slack = jnp.minimum(source_of - 1, most - receiver)
    passed = jax.random.randint(jax.random.fold_in(stream_key, 1), (pairs,), 0, 1 << 20) % (slack + 1)
    lengths = lengths.at[1:1 + 2 * pairs:2].set(source_of - passed).at[2:2 + 2 * pairs:2].set(receiver + passed)
    return lengths[jax.random.permutation(jax.random.fold_in(stream_key, 2), number_of)]


def bell_draw(key, extent, deviation, reach, cuts=(), kind=jnp.bfloat16):
    gain = block_levels(key, extent, cuts, -0.22, 0.18) if cuts else 1.0
    values = jax.random.normal(key, extent, jnp.float32) * deviation * gain
    return jnp.minimum(jnp.maximum(values, -reach), reach).astype(kind)


def setup_inputs(seed: int = 0) -> dict:
    seeds = jax.random.split(jax.random.key(seed), 19)
    return {
        "inputs": bell_draw(seeds[0], (SEQS, LEN, D), 1.0, 6.0, ((0, 8), (1, 4))),
        "block_ids": jax.vmap(lambda own: jnp.searchsorted(jnp.cumsum(uneven(own, 2, NBLK, NBLK - NBLK // 4, 0)), jnp.arange(NBLK), side="right"))(jax.random.split(seeds[1], SEQS)).reshape((SEQS, NBLK)).astype(jnp.int32),
        "query_weight": bell_draw(seeds[2], (D, D), (D // 2) ** -0.5, 0.3125, ((0, 8),)),
        "query_bias": bell_draw(seeds[3], (D,), 0.5, 3.0, ((0, 8),)),
        "key_weight": bell_draw(seeds[4], (D, D), (D // 2) ** -0.5, 0.3125, ((0, 8),)),
        "value_weight": bell_draw(seeds[5], (D, D), D ** -0.5, 0.21875, ((0, 8),)),
        "value_bias": bell_draw(seeds[6], (D,), 0.5, 3.0, ((0, 8),)),
        "output_weight": bell_draw(seeds[7], (D, D), (D // 32) ** -0.5, 1.25, ((0, 8),)),
        "output_bias": bell_draw(seeds[8], (D,), 0.5, 3.0, ((0, 8),)),
        "attention_gain": jnp.clip(1.0 + 0.1 * jax.random.normal(seeds[9], (D,), jnp.float32), 0.5, 1.5).astype(jnp.bfloat16),
        "attention_shift": bell_draw(seeds[10], (D,), 0.3, 2.0, ((0, 8),)),
        "expand_weight": bell_draw(seeds[11], (D, FF), D ** -0.5, 0.21875, ((0, 8),)),
        "expand_bias": bell_draw(seeds[12], (FF,), 0.5, 3.0, ((0, 8),)),
        "reduce_weight": bell_draw(seeds[13], (FF, D), FF ** -0.5, 0.109375, ((0, 8),)),
        "reduce_bias": bell_draw(seeds[14], (D,), 0.5, 3.0, ((0, 8),)),
        "final_gain": jnp.clip(1.0 + 0.1 * jax.random.normal(seeds[15], (D,), jnp.float32), 0.5, 1.5).astype(jnp.bfloat16),
        "final_shift": bell_draw(seeds[16], (D,), 0.3, 2.0, ((0, 8),)),
        "cotangent": bell_draw(seeds[17], (SEQS, LEN, D), 1.0, 6.0, ((0, 8), (1, 4))),
    }


@jax.custom_vjp
def low(v):
    return lax.optimization_barrier(v.astype(jnp.bfloat16)).astype(jnp.float32)

@jax.custom_vjp
def low_back(v):
    return v

def low_keep(v):
    return (low(v), None)

def low_pass(kept, grad):
    return (grad,)

def back_keep(v):
    return (v, None)

def back_low(kept, grad):
    return (low(grad),)
low.defvjp(low_keep, low_pass)
low_back.defvjp(back_keep, back_low)
EPSILON = 1e-12
MASKED = -1e+30
HIGHEST = lax.Precision.HIGHEST

def product(former, latter):
    return jnp.dot(former, latter, precision=HIGHEST)

def layer_norm(values, norm_gain, norm_shift):
    middle = lax.optimization_barrier(jnp.mean(values, axis=-1, keepdims=True))
    centred = values - middle
    spread = lax.optimization_barrier(jnp.mean(centred * centred, axis=-1, keepdims=True))
    return centred * lax.rsqrt(spread + EPSILON) * norm_gain + norm_shift

def attention(queries, key_rows, value_rows, token_doc):
    row_count = min(512, LEN)
    query_heads = queries.reshape(LEN, HEADS, HD)
    key_heads = key_rows.reshape(LEN, HEADS, HD)
    value_heads = value_rows.reshape(LEN, HEADS, HD)
    positions = jnp.arange(LEN, dtype=jnp.int32)

    def one_block(row_start):
        block_queries = lax.dynamic_slice_in_dim(query_heads, row_start, row_count, 0)
        block_docs = lax.dynamic_slice_in_dim(token_doc, row_start, row_count, 0)
        block_rows = row_start + jnp.arange(row_count, dtype=jnp.int32)
        allowed = (block_docs[:, None] == token_doc[None, :]) & (positions[None, :] // BLK <= block_rows[:, None] // BLK)
        scores = jnp.einsum('qhd,khd->hqk', block_queries, key_heads, precision=HIGHEST) * HD ** (-0.5)
        scores = low_back(scores)
        scores = jnp.where(allowed[None], scores, MASKED)
        row_peak = lax.optimization_barrier(jnp.max(scores, axis=-1, keepdims=True))
        exponent = jnp.exp(scores - row_peak)
        probabilities = low(exponent / lax.optimization_barrier(jnp.sum(exponent, axis=-1, keepdims=True)))
        return jnp.einsum('hqk,khd->qhd', probabilities, value_heads, precision=HIGHEST)
    starts = jnp.arange(LEN // row_count, dtype=jnp.int32) * row_count
    blocks = lax.map(jax.checkpoint(one_block), starts)
    return blocks.reshape(LEN, D)

def forward(tokens, query_weight, query_bias, key_weight, value_weight, value_bias, output_weight, output_bias, attention_gain, attention_shift, expand_weight, expand_bias, reduce_weight, reduce_bias, final_gain, final_shift, token_doc):
    queries = low_back(low(product(tokens, query_weight) + query_bias))
    key_rows = low_back(low(product(tokens, key_weight)))
    value_rows = low_back(low(product(tokens, value_weight) + value_bias))
    context = low_back(low(attention(queries, key_rows, value_rows, token_doc)))
    attended = low_back(product(context, output_weight) + output_bias)
    hidden = low(layer_norm(tokens + attended, attention_gain, attention_shift))
    expanded = low_back(product(hidden, expand_weight) + expand_bias)
    activated = low(jax.nn.gelu(expanded, approximate=False))
    reduced = low_back(product(activated, reduce_weight) + reduce_bias)
    return layer_norm(hidden + reduced, final_gain, final_shift)

def reference(inputs, block_ids, query_weight, query_bias, key_weight, value_weight, value_bias, output_weight, output_bias, attention_gain, attention_shift, expand_weight, expand_bias, reduce_weight, reduce_bias, final_gain, final_shift, cotangent):
    params = tuple((array_item.astype(jnp.float32) for array_item in (query_weight, query_bias, key_weight, value_weight, value_bias, output_weight, output_bias, attention_gain, attention_shift, expand_weight, expand_bias, reduce_weight, reduce_bias, final_gain, final_shift)))

    def one_sequence(running_sums, sequence_item):
        sequence_tokens, sequence_blocks, sequence_tangent = sequence_item
        token_doc = jnp.repeat(sequence_blocks.astype(jnp.int32), BLK, total_repeat_length=LEN)

        def apply_layer(tokens, *weights):
            return forward(tokens, *weights, token_doc)
        result, pullback = jax.vjp(apply_layer, sequence_tokens.astype(jnp.float32), *params)
        gradients = pullback(sequence_tangent.astype(jnp.float32))
        running_sums = tuple((running + change for running, change in zip(running_sums, gradients[1:])))
        return (running_sums, (result.astype(jnp.bfloat16), gradients[0]))
    zeros_start = tuple((jnp.zeros(array_item.shape, jnp.float32) for array_item in params))
    layer_sums, (output, input_gradient) = lax.scan(one_sequence, zeros_start, (inputs, block_ids, cotangent))
    query_matrix, query_vector, key_matrix, value_matrix, value_vector, output_matrix, output_vector, first_scale, first_offset, expand_matrix, expand_vector, reduce_matrix, reduce_vector, last_scale, last_offset = layer_sums
    return (output, input_gradient, query_matrix, query_vector, key_matrix, value_matrix, value_vector, output_matrix, output_vector, first_scale, first_offset, expand_matrix, expand_vector, reduce_matrix, reduce_vector, last_scale, last_offset)
```

```python
import functools

import jax
import jax.numpy as jnp
from jax import lax
from jax.experimental import pallas as pl
from jax.experimental.pallas import tpu as pltpu
from jax.sharding import PartitionSpec as P

HD = 64
BLK = 256


EPSILON = 1e-12
MASKED = -1e30
ROW_BLOCK = 512


def as_sent(value):
    return jax.tree.map(lambda a: a.astype(jnp.bfloat16) if a.dtype == jnp.float32 else a, value)


def layer_norm(values, norm_gain, norm_shift):
    middle = jnp.mean(values, axis=-1, keepdims=True)
    centred = values - middle
    spread = jnp.mean(centred * centred, axis=-1, keepdims=True)
    return centred * lax.rsqrt(spread + EPSILON) * norm_gain + norm_shift


def gelu_exact(values):
    return jax.nn.gelu(values, approximate=False)


def product(former, latter):
    return jnp.dot(former, latter, preferred_element_type=jnp.float32)


def left_transposed(former, latter):
    return lax.dot_general(
        former, latter, (((0,), (0,)), ((), ())), preferred_element_type=jnp.float32
    )


def right_transposed(former, latter):
    return lax.dot_general(
        former, latter, (((1,), (1,)), ((), ())), preferred_element_type=jnp.float32
    )


def column_sum(values):
    return jnp.sum(values.astype(jnp.float32), axis=0)


def block_mask(allowed, row_start, row_count, key_reach):
    table_part = allowed[row_start // BLK : (row_start + row_count) // BLK, : key_reach // BLK]
    return jnp.repeat(jnp.repeat(table_part, BLK, axis=0), BLK, axis=1)


def masked_scores(queries, key_rows, allowed, row_start, row_count):
    key_reach = row_start + row_count
    scores = right_transposed(queries[row_start:key_reach], key_rows[:key_reach]) * HD ** (-0.5)
    return jnp.where(block_mask(allowed, row_start, row_count, key_reach), scores, MASKED)


def head_forward(head_item, allowed):
    queries, key_rows, value_rows = head_item
    length = queries.shape[0]
    row_count = min(ROW_BLOCK, length)
    contexts = []
    totals = []
    for row_start in range(0, length, row_count):
        scores = masked_scores(queries, key_rows, allowed, row_start, row_count)
        row_peak = jnp.max(scores, axis=-1, keepdims=True)
        exponent = jnp.exp(scores - row_peak)
        row_total = jnp.sum(exponent, axis=-1, keepdims=True)
        probabilities = (exponent / row_total).astype(jnp.bfloat16)
        contexts.append(
            product(probabilities, value_rows[: row_start + row_count]).astype(jnp.bfloat16)
        )
        totals.append(row_peak[:, 0] + jnp.log(row_total[:, 0]))
    return (jnp.concatenate(contexts, axis=0), jnp.concatenate(totals, axis=0))


def head_backward(head_item, allowed):
    queries, key_rows, value_rows, context_rows, totals = head_item
    length = queries.shape[0]
    row_count = min(ROW_BLOCK, length)
    score_scale = HD ** (-0.5)
    query_parts = []
    key_total = jnp.zeros(key_rows.shape, jnp.float32)
    value_total = jnp.zeros(value_rows.shape, jnp.float32)
    for row_start in range(0, length, row_count):
        key_reach = row_start + row_count
        scores = masked_scores(queries, key_rows, allowed, row_start, row_count)
        probabilities = jnp.exp(scores - totals[row_start:key_reach, None])
        incoming = context_rows[row_start:key_reach]
        back_weights = right_transposed(incoming, value_rows[:key_reach])
        inner_sum = jnp.sum(probabilities * back_weights, axis=-1, keepdims=True)
        back_scores = (probabilities * (back_weights - inner_sum)).astype(jnp.bfloat16)
        query_parts.append(product(back_scores, key_rows[:key_reach]) * score_scale)
        key_total = key_total.at[:key_reach].add(
            left_transposed(back_scores, queries[row_start:key_reach]) * score_scale
        )
        value_total = value_total.at[:key_reach].add(
            left_transposed(probabilities.astype(jnp.bfloat16), incoming)
        )
    back_queries = jnp.concatenate(query_parts, axis=0).astype(jnp.bfloat16)
    return (back_queries, key_total.astype(jnp.bfloat16), value_total.astype(jnp.bfloat16))


def general_shards(
    inputs,
    block_ids,
    query_weight,
    query_bias,
    key_weight,
    value_weight,
    value_bias,
    output_weight,
    output_bias,
    attention_gain,
    attention_shift,
    expand_weight,
    expand_bias,
    reduce_weight,
    reduce_bias,
    final_gain,
    final_shift,
    cotangent,
):
    tokens = inputs[0]
    documents = block_ids[0]
    block_order = jnp.arange(documents.shape[0], dtype=jnp.int32)
    allowed = (documents[:, None] == documents[None, :]) & (
        block_order[None, :] <= block_order[:, None]
    )
    (
        query_full,
        query_shift,
        key_full,
        value_full,
        value_shift,
        output_full,
        output_shift,
        norm_gain,
        norm_shift,
        expand_full,
        expand_shift,
        reduce_full,
        reduce_shift,
        last_gain,
        last_shift,
    ) = (
        lax.all_gather(query_weight, "dp", axis=0, tiled=True),
        lax.all_gather(query_bias, "dp", axis=0, tiled=True),
        lax.all_gather(key_weight, "dp", axis=0, tiled=True),
        lax.all_gather(value_weight, "dp", axis=0, tiled=True),
        lax.all_gather(value_bias, "dp", axis=0, tiled=True),
        lax.all_gather(output_weight, "dp", axis=0, tiled=True),
        lax.all_gather(output_bias, "dp", axis=0, tiled=True),
        lax.all_gather(attention_gain, "dp", axis=0, tiled=True),
        lax.all_gather(attention_shift, "dp", axis=0, tiled=True),
        lax.all_gather(expand_weight, "dp", axis=0, tiled=True),
        lax.all_gather(expand_bias, "dp", axis=0, tiled=True),
        lax.all_gather(reduce_weight, "dp", axis=0, tiled=True),
        lax.all_gather(reduce_bias, "dp", axis=0, tiled=True),
        lax.all_gather(final_gain, "dp", axis=0, tiled=True),
        lax.all_gather(final_shift, "dp", axis=0, tiled=True),
    )
    queries_token = (product(tokens, query_full) + query_shift.astype(jnp.float32)).astype(
        jnp.bfloat16
    )
    keys_token = product(tokens, key_full).astype(jnp.bfloat16)
    values_token = (product(tokens, value_full) + value_shift.astype(jnp.float32)).astype(
        jnp.bfloat16
    )
    stacked = jnp.stack([queries_token, keys_token, values_token])
    spread_heads = lax.all_to_all(stacked, "seq", split_axis=2, concat_axis=1, tiled=True)
    length = spread_heads.shape[1]
    head_count = spread_heads.shape[2] // HD
    by_head = spread_heads.reshape(3, length, head_count, HD).transpose(0, 2, 1, 3)
    contexts, totals = lax.map(
        lambda head_item: head_forward(head_item, allowed), (by_head[0], by_head[1], by_head[2])
    )
    context_rows = contexts.transpose(1, 0, 2).reshape(length, head_count * HD)
    context_token = lax.all_to_all(
        as_sent(context_rows), "seq", split_axis=0, concat_axis=1, tiled=True
    ).astype(context_rows.dtype)
    attended = product(context_token, output_full) + output_shift.astype(jnp.float32)
    first_pre = tokens.astype(jnp.float32) + attended
    hidden, first_pull = jax.vjp(
        layer_norm, first_pre, norm_gain.astype(jnp.float32), norm_shift.astype(jnp.float32)
    )
    hidden_low = hidden.astype(jnp.bfloat16)
    expanded = product(hidden_low, expand_full) + expand_shift.astype(jnp.float32)
    activated, gelu_pull = jax.vjp(gelu_exact, expanded)
    activated_low = activated.astype(jnp.bfloat16)
    reduced = product(activated_low, reduce_full) + reduce_shift.astype(jnp.float32)
    final_pre = hidden_low.astype(jnp.float32) + reduced
    final_out, final_pull = jax.vjp(
        layer_norm, final_pre, last_gain.astype(jnp.float32), last_shift.astype(jnp.float32)
    )
    output = final_out.astype(jnp.bfloat16)[None]
    query_full, key_full, value_full, output_full, expand_full, reduce_full = (
        lax.all_gather(query_weight, "dp", axis=0, tiled=True),
        lax.all_gather(key_weight, "dp", axis=0, tiled=True),
        lax.all_gather(value_weight, "dp", axis=0, tiled=True),
        lax.all_gather(output_weight, "dp", axis=0, tiled=True),
        lax.all_gather(expand_weight, "dp", axis=0, tiled=True),
        lax.all_gather(reduce_weight, "dp", axis=0, tiled=True),
    )
    back_final, last_scale, last_offset = final_pull(cotangent[0].astype(jnp.float32))
    back_reduced = back_final.astype(jnp.bfloat16)
    reduce_matrix = left_transposed(activated_low, back_reduced)
    reduce_vector = column_sum(back_reduced)
    back_activated = right_transposed(back_reduced, reduce_full)
    back_expanded = gelu_pull(back_activated)[0].astype(jnp.bfloat16)
    expand_matrix = left_transposed(hidden_low, back_expanded)
    expand_vector = column_sum(back_expanded)
    back_hidden = back_final + right_transposed(back_expanded, expand_full)
    back_attended, first_scale, first_offset = first_pull(back_hidden)
    attended_low = back_attended.astype(jnp.bfloat16)
    output_matrix = left_transposed(context_token, attended_low)
    output_vector = column_sum(attended_low)
    back_context = right_transposed(attended_low, output_full).astype(jnp.bfloat16)
    context_spread = lax.all_to_all(back_context, "seq", split_axis=1, concat_axis=0, tiled=True)
    context_by_head = context_spread.reshape(length, head_count, HD).transpose(1, 0, 2)
    back_heads = lax.map(
        lambda head_item: head_backward(head_item, allowed),
        (by_head[0], by_head[1], by_head[2], context_by_head, totals),
    )
    back_stacked = jnp.stack(back_heads).transpose(0, 2, 1, 3).reshape(3, length, head_count * HD)
    back_token = lax.all_to_all(
        as_sent(back_stacked), "seq", split_axis=1, concat_axis=2, tiled=True
    ).astype(back_stacked.dtype)
    back_query = back_token[0]
    back_key = back_token[1]
    back_value = back_token[2]
    input_gradient = (
        back_attended
        + right_transposed(back_query, query_full)
        + right_transposed(back_key, key_full)
        + right_transposed(back_value, value_full)
    )
    query_matrix = left_transposed(tokens, back_query)
    query_vector = column_sum(back_query)
    key_matrix = left_transposed(tokens, back_key)
    value_matrix = left_transposed(tokens, back_value)
    value_vector = column_sum(back_value)
    (
        query_matrix,
        query_vector,
        key_matrix,
        value_matrix,
        value_vector,
        output_matrix,
        output_vector,
        first_scale,
        first_offset,
        expand_matrix,
        expand_vector,
        reduce_matrix,
        reduce_vector,
        last_scale,
        last_offset,
    ) = (
        lax.psum_scatter(query_matrix, "dp", scatter_dimension=0, tiled=True),
        lax.psum_scatter(query_vector, "dp", scatter_dimension=0, tiled=True),
        lax.psum_scatter(key_matrix, "dp", scatter_dimension=0, tiled=True),
        lax.psum_scatter(value_matrix, "dp", scatter_dimension=0, tiled=True),
        lax.psum_scatter(value_vector, "dp", scatter_dimension=0, tiled=True),
        lax.psum_scatter(output_matrix, "dp", scatter_dimension=0, tiled=True),
        lax.psum_scatter(output_vector, "dp", scatter_dimension=0, tiled=True),
        lax.psum_scatter(first_scale, "dp", scatter_dimension=0, tiled=True),
        lax.psum_scatter(first_offset, "dp", scatter_dimension=0, tiled=True),
        lax.psum_scatter(expand_matrix, "dp", scatter_dimension=0, tiled=True),
        lax.psum_scatter(expand_vector, "dp", scatter_dimension=0, tiled=True),
        lax.psum_scatter(reduce_matrix, "dp", scatter_dimension=0, tiled=True),
        lax.psum_scatter(reduce_vector, "dp", scatter_dimension=0, tiled=True),
        lax.psum_scatter(last_scale, "dp", scatter_dimension=0, tiled=True),
        lax.psum_scatter(last_offset, "dp", scatter_dimension=0, tiled=True),
    )
    owned = (
        lax.psum(query_matrix.astype(jnp.bfloat16), "seq").astype(jnp.float32),
        lax.psum(query_vector.astype(jnp.bfloat16), "seq").astype(jnp.float32),
        lax.psum(key_matrix.astype(jnp.bfloat16), "seq").astype(jnp.float32),
        lax.psum(value_matrix.astype(jnp.bfloat16), "seq").astype(jnp.float32),
        lax.psum(value_vector.astype(jnp.bfloat16), "seq").astype(jnp.float32),
        lax.psum(output_matrix.astype(jnp.bfloat16), "seq").astype(jnp.float32),
        lax.psum(output_vector.astype(jnp.bfloat16), "seq").astype(jnp.float32),
        lax.psum(first_scale.astype(jnp.bfloat16), "seq").astype(jnp.float32),
        lax.psum(first_offset.astype(jnp.bfloat16), "seq").astype(jnp.float32),
        lax.psum(expand_matrix.astype(jnp.bfloat16), "seq").astype(jnp.float32),
        lax.psum(expand_vector.astype(jnp.bfloat16), "seq").astype(jnp.float32),
        lax.psum(reduce_matrix.astype(jnp.bfloat16), "seq").astype(jnp.float32),
        lax.psum(reduce_vector.astype(jnp.bfloat16), "seq").astype(jnp.float32),
        lax.psum(last_scale.astype(jnp.bfloat16), "seq").astype(jnp.float32),
        lax.psum(last_offset.astype(jnp.bfloat16), "seq").astype(jnp.float32),
    )
    return (output, input_gradient[None]) + tuple(owned)


MESH = pl.DeviceIdType.MESH
KEY, VALUE, QUERY, OUT, EXPAND, REDUCE = range(6)
ROWS = (96, 96, 96, 96, 96, 384)
COLS = (768, 768, 768, 768, 3072, 768)
GATHER_UNITS = (
    [(w, 0, 768, False) for w in (KEY, VALUE, QUERY, OUT)]
    + [(EXPAND, 768 * j, 768, True) for j in range(4)]
    + [(REDUCE, 256 * j, 256, True) for j in range(3)]
)
SUM_UNITS = (
    [(REDUCE, 256 * j, 256) for j in range(3)]
    + [(EXPAND, 768 * j, 768) for j in range(4)]
    + [(w, 0, 768) for w in (OUT, QUERY, KEY, VALUE)]
)
TOKENS = 256
WIDTH = 768


class Place:
    def __init__(self):
        self.d = lax.axis_index("dp")
        self.z = lax.axis_index("seq")
        self.y = self.d // 4
        self.x = (self.d // 2) % 2
        self.c = self.d % 2
        self.parity = self.z % 2
        self.partner_z = self.z + 1 - 2 * self.parity

    def shard(self, flip_y, flip_x, flip_c):
        y = 1 - self.y if flip_y else self.y
        x = 1 - self.x if flip_x else self.x
        c = 1 - self.c if flip_c else self.c
        return 4 * y + 2 * x + c

    def quarter(self, flip_y, flip_x):
        y = 1 - self.y if flip_y else self.y
        x = 1 - self.x if flip_x else self.x
        return 2 * y + x

    def peer(self, kind):
        if kind == "x":
            return (self.shard(0, 1, 0), self.z)
        if kind == "y":
            return (self.shard(1, 0, 0), self.z)
        if kind == "s":
            return (self.shard(0, 0, 1), self.z)
        return (self.d, self.partner_z)


def remote(source, target, send_sem, recv_sem, peer):
    return pltpu.make_async_remote_copy(
        src_ref=source,
        dst_ref=target,
        send_sem=send_sem,
        recv_sem=recv_sem,
        device_id=peer,
        device_id_type=MESH,
    )


class Gather:
    def __init__(self, place, own, full, send_sems, recv_sems):
        self.place, self.own, self.full = place, own, full
        self.send_sems, self.recv_sems = send_sems, recv_sems

    def rows(self, unit, part):
        w, _, _, paired = GATHER_UNITS[unit]
        count = ROWS[w]
        parity = self.place.parity
        if part == "all":
            return pl.ds(0, count)
        if not paired:
            half = count // 2
            return {"a": pl.ds(0, half), "b": pl.ds(half, half), "ab": pl.ds(0, count)}[part]
        third = count // 3
        if part == "a":
            return pl.ds(pl.multiple_of(2 * third * parity, third), third)
        if part == "b":
            return pl.ds(third, third)
        if part == "w":
            return pl.ds(pl.multiple_of(2 * third * (1 - parity), third), third)
        return pl.ds(pl.multiple_of(third * parity, third), 2 * third)

    def slot(self, unit, shard, part):
        w, col, width, _ = GATHER_UNITS[unit]
        return self.full[w].at[shard, self.rows(unit, part), pl.ds(col, width)]

    def copy(self, unit, lane, kind, shard, part, source=None):
        target = self.slot(unit, shard, part)
        return remote(
            target if source is None else source,
            target,
            self.send_sems.at[unit, lane],
            self.recv_sems.at[unit, lane],
            self.place.peer(kind),
        )

    def own_source(self, unit, part):
        w, col, width, _ = GATHER_UNITS[unit]
        return self.own[w].at[self.rows(unit, part), pl.ds(col, width)]

    def sends(self, unit):
        p = self.place
        mine, over_x, over_y, over_d = p.d, p.shard(0, 1, 0), p.shard(1, 0, 0), p.shard(1, 1, 0)
        table = {
            0: ("x", mine, "ab", True),
            1: ("x", over_y, "a", False),
            2: ("y", mine, "ab", True),
            3: ("y", over_x, "b", False),
            4: ("s", mine, "all", True),
            5: ("s", over_x, "ab", False),
            6: ("s", over_y, "ab", False),
            7: ("s", over_d, "ab", False),
        }
        if GATHER_UNITS[unit][3]:
            table.update(
                {
                    8: ("z", over_x, "a", False),
                    9: ("z", over_y, "a", False),
                    10: ("z", over_d, "a", False),
                    11: ("s", over_x, "w", False),
                    12: ("s", over_y, "w", False),
                    13: ("s", over_d, "w", False),
                }
            )
        return table

    def arrivals(self, unit):
        p = self.place
        over_x, over_y, over_d = p.shard(0, 1, 0), p.shard(1, 0, 0), p.shard(1, 1, 0)
        sib, sib_x, sib_y, sib_d = p.shard(0, 0, 1), p.shard(0, 1, 1), p.shard(1, 0, 1), p.shard(1, 1, 1)
        return {
            0: ("x", over_x, "ab"),
            1: ("x", over_d, "a"),
            2: ("y", over_y, "ab"),
            3: ("y", over_d, "b"),
            4: ("s", sib, "all"),
            5: ("s", sib_x, "ab"),
            6: ("s", sib_y, "ab"),
            7: ("s", sib_d, "ab"),
            8: ("z", over_x, "w"),
            9: ("z", over_y, "w"),
            10: ("z", over_d, "w"),
            11: ("s", sib_x, "w"),
            12: ("s", sib_y, "w"),
            13: ("s", sib_d, "w"),
        }

    def start(self, unit, *lanes):
        table = self.sends(unit)
        for lane in lanes:
            if lane in table:
                kind, shard, part, from_own = table[lane]
                source = self.own_source(unit, part) if from_own else None
                self.copy(unit, lane, kind, shard, part, source).start()

    def wait(self, unit, *lanes):
        table = self.sends(unit)
        for lane in lanes:
            if lane in table:
                kind, shard, part = self.arrivals(unit)[lane]
                self.copy(unit, lane, kind, shard, part).wait_recv()

    def open(self, unit):
        if unit < len(GATHER_UNITS):
            self.start(unit, 0, 2, 4)

    def relay(self, unit):
        if 0 <= unit < len(GATHER_UNITS):
            self.wait(unit, 0)
            self.start(unit, 3, 8, 5)
            self.wait(unit, 2)
            self.start(unit, 1, 9, 6)

    def relay_far(self, unit):
        if 0 <= unit < len(GATHER_UNITS):
            self.wait(unit, 1)
            self.start(unit, 10)
            self.wait(unit, 3)
            self.start(unit, 7)
            self.wait(unit, 8)
            self.start(unit, 11)
            self.wait(unit, 9)
            self.start(unit, 12)

    def relay_last(self, unit):
        if 0 <= unit < len(GATHER_UNITS):
            self.wait(unit, 10)
            self.start(unit, 13)

    def arrived(self, unit):
        if 0 <= unit < len(GATHER_UNITS):
            self.wait(unit, 4, 5, 6, 7, 11, 12, 13)

    def drain(self):
        for unit in range(len(GATHER_UNITS)):
            for lane, (kind, shard, part, from_own) in self.sends(unit).items():
                source = self.own_source(unit, part) if from_own else None
                self.copy(unit, lane, kind, shard, part, source).wait_send()


PLANE = [(fy, fx, fc) for fy in (0, 1) for fx in (0, 1) for fc in (0, 1)][1:]


def greet(place):
    barrier = pltpu.get_barrier_semaphore()
    for flips in PLANE:
        pl.semaphore_signal(
            barrier, inc=1, device_id=(place.shard(*flips), place.z), device_id_type=MESH
        )

    @pl.when(place.z > 0)
    def _():
        pl.semaphore_signal(barrier, inc=1, device_id=(place.d, place.z - 1), device_id_type=MESH)

    @pl.when(place.z < 3)
    def _():
        pl.semaphore_signal(barrier, inc=1, device_id=(place.d, place.z + 1), device_id_type=MESH)

    pl.semaphore_wait(barrier, 8 + (place.z * (3 - place.z)) // 2)


def gather_kernel(*refs):
    own = refs[:6]
    vectors, tokens = refs[6:8]
    full = refs[8:14]
    all_vectors, blocks = refs[14:16]
    local_sems, send_sems, recv_sems, vec_send, vec_recv, tok_send, tok_recv = refs[16:]
    place = Place()
    gather = Gather(place, own, full, send_sems, recv_sems)
    greet(place)
    gather.open(0)
    gather.open(1)

    def vector_copy(i, shard, peer):
        return remote(vectors, all_vectors.at[shard], vec_send.at[i], vec_recv.at[i], peer)

    for i, flips in enumerate(PLANE):
        vector_copy(i, place.d, (place.shard(*flips), place.z)).start()

    def token_copy(slot, source, peer_z):
        return remote(
            source, blocks.at[slot], tok_send.at[slot], tok_recv.at[slot], (place.d, peer_z)
        )

    @pl.when(place.z < 3)
    def _():
        token_copy(1, tokens.at[0], place.z + 1).start()

    @pl.when(place.z == 0)
    def _():
        blocks[0] = jnp.zeros((TOKENS, WIDTH), jnp.bfloat16)
        blocks[1] = jnp.zeros((TOKENS, WIDTH), jnp.bfloat16)

    @pl.when(place.z == 1)
    def _():
        blocks[0] = jnp.zeros((TOKENS, WIDTH), jnp.bfloat16)

    local = [pltpu.make_async_copy(own[w], full[w].at[place.d], local_sems.at[w]) for w in range(6)]
    local.append(pltpu.make_async_copy(vectors, all_vectors.at[place.d], local_sems.at[6]))
    local.append(pltpu.make_async_copy(tokens.at[0], blocks.at[2], local_sems.at[7]))
    for copy in local:
        copy.start()

    units = len(GATHER_UNITS)
    for unit in range(units + 3):
        if unit == 1:
            @pl.when(place.z > 0)
            def _():
                token_copy(1, tokens.at[0], place.z - 1).wait_recv()

                @pl.when(place.z < 3)
                def _():
                    token_copy(0, blocks.at[1], place.z + 1).start()

        gather.relay(unit)
        gather.open(unit + 2)
        gather.relay_far(unit - 1)
        gather.relay_last(unit - 2)
        gather.arrived(unit - 3)

    @pl.when(place.z > 1)
    def _():
        token_copy(0, blocks.at[1], place.z - 1).wait_recv()

    for i, flips in enumerate(PLANE):
        vector_copy(i, place.shard(*flips), (place.shard(*flips), place.z)).wait_recv()
    for copy in local:
        copy.wait()
    gather.drain()
    for i, flips in enumerate(PLANE):
        vector_copy(i, place.d, (place.shard(*flips), place.z)).wait_send()

    @pl.when(place.z < 3)
    def _():
        token_copy(1, tokens.at[0], place.z + 1).wait_send()

    @pl.when((place.z > 0) & (place.z < 3))
    def _():
        token_copy(0, blocks.at[1], place.z + 1).wait_send()


def gather_call(weights, vectors, tokens):
    hbm = pl.BlockSpec(memory_space=pl.ANY)
    vmem = pl.BlockSpec(memory_space=pltpu.VMEM)
    units = len(GATHER_UNITS)
    dma = pltpu.SemaphoreType.DMA
    return pl.pallas_call(
        gather_kernel,
        out_shape=[
            jax.ShapeDtypeStruct((8, ROWS[w], COLS[w]), jnp.bfloat16) for w in range(6)
        ]
        + [
            jax.ShapeDtypeStruct((8, 16, 128), jnp.bfloat16),
            jax.ShapeDtypeStruct((3, TOKENS, WIDTH), jnp.bfloat16),
        ],
        in_specs=[hbm] * 8,
        out_specs=[vmem] * 8,
        scratch_shapes=[
            dma((8,)),
            dma((units, 14)),
            dma((units, 14)),
            dma((7,)),
            dma((7,)),
            dma((2,)),
            dma((2,)),
        ],
        compiler_params=pltpu.CompilerParams(
            collective_id=0, has_side_effects=True, vmem_limit_bytes=60 << 20
        ),
        name="gather_weights",
    )(*weights, vectors, tokens)


def cut(unit, part):
    count = ROWS[SUM_UNITS[unit][0]]
    half = count // 2
    return {"a": pl.ds(0, half), "b": pl.ds(half, half), "all": pl.ds(0, count)}[part]


class Reduce:
    def __init__(self, place, buffers, send_sems, recv_sems):
        self.place = place
        self.sib, self.chip, self.far, self.near, self.plane = buffers[:5]
        self.outer, self.half, self.inner, self.total = buffers[5:]
        self.send_sems, self.recv_sems = send_sems, recv_sems
        self.rim_z = jnp.where(place.z < 2, 0, 3)
        self.core_z = jnp.where(place.z < 2, 1, 2)
        self.is_rim = (place.z == 0) | (place.z == 3)

    def view(self, family, unit, part, *lead):
        w, col, width = SUM_UNITS[unit]
        return family[w].at[(*lead, cut(unit, part), pl.ds(col, width))]

    def copy(self, unit, lane, source, target, peer):
        return remote(
            source, target, self.send_sems.at[unit, lane], self.recv_sems.at[unit, lane], peer
        )

    def sibling(self, unit, source):
        w, col, width = SUM_UNITS[unit]
        return self.copy(
            unit, 0, source, self.sib[w].at[:, :, pl.ds(col, width)], self.place.peer("s")
        )

    def lanes(self, unit):
        p = self.place
        to_x, to_y, to_d = p.quarter(0, 1), p.quarter(1, 0), p.quarter(1, 1)
        c, f, n = self.chip, self.far, self.near
        x, y = p.peer("x"), p.peer("y")
        return {
            1: (self.view(c, unit, "a", to_d), self.view(f, unit, "a"), x),
            2: (self.view(c, unit, "b", to_d), self.view(f, unit, "b"), y),
            3: (self.view(c, unit, "a", to_x), self.view(n, unit, "a", 0), x),
            4: (self.view(c, unit, "b", to_x), self.view(n, unit, "b", 0), x),
            5: (self.view(c, unit, "b", to_y), self.view(n, unit, "b", 1), y),
            6: (self.view(c, unit, "a", to_y), self.view(n, unit, "a", 1), y),
            7: (
                self.view(self.plane, unit, "all"),
                self.view(self.outer, unit, "all"),
                (p.d, self.core_z),
            ),
            8: (
                self.view(self.half, unit, "all"),
                self.view(self.inner, unit, "all"),
                (p.d, 3 - self.core_z),
            ),
            9: (
                self.view(self.total, unit, "all"),
                self.view(self.total, unit, "all"),
                (p.d, self.rim_z),
            ),
        }

    def start(self, unit, *lanes):
        table = self.lanes(unit)
        for lane in lanes:
            self.copy(unit, lane, *table[lane]).start()

    def wait(self, unit, *lanes):
        table = self.lanes(unit)
        for lane in lanes:
            self.copy(unit, lane, *table[lane]).wait_recv()

    def chip_sum(self, unit, own):
        if not 0 <= unit < len(SUM_UNITS):
            return
        w, col, width = SUM_UNITS[unit]
        self.sibling(unit, self.sib[w].at[:, :, pl.ds(col, width)]).wait_recv()
        for quarter in range(4):
            term = own(quarter) + self.view(self.sib, unit, "all", quarter)[...].astype(jnp.float32)
            self.view(self.chip, unit, "all", quarter)[...] = term.astype(jnp.bfloat16)
        self.start(unit, 1, 2, 3, 5)

    def relay(self, unit):
        if not 0 <= unit < len(SUM_UNITS):
            return
        p = self.place
        for lane, part, quarter, after in (
            (1, "a", p.quarter(1, 0), 6),
            (2, "b", p.quarter(0, 1), 4),
        ):
            self.wait(unit, lane)
            target = self.view(self.chip, unit, part, quarter)
            target[...] = (
                target[...].astype(jnp.float32)
                + self.view(self.far, unit, part)[...].astype(jnp.float32)
            ).astype(jnp.bfloat16)
            self.start(unit, after)

    def plane_sum(self, unit):
        if not 0 <= unit < len(SUM_UNITS):
            return
        mine = self.place.quarter(0, 0)
        self.wait(unit, 3, 4, 5, 6)
        total = self.view(self.chip, unit, "all", mine)[...].astype(jnp.float32)
        for side in (0, 1):
            total = total + self.view(self.near, unit, "all", side)[...].astype(jnp.float32)
        self.view(self.plane, unit, "all")[...] = total.astype(jnp.bfloat16)

        @pl.when(self.is_rim)
        def _():
            self.start(unit, 7)

    def half_sum(self, unit):
        if not 0 <= unit < len(SUM_UNITS):
            return

        @pl.when(jnp.logical_not(self.is_rim))
        def _():
            self.wait(unit, 7)
            self.view(self.half, unit, "all")[...] = (
                self.view(self.plane, unit, "all")[...].astype(jnp.float32)
                + self.view(self.outer, unit, "all")[...].astype(jnp.float32)
            ).astype(jnp.bfloat16)
            self.start(unit, 8)

    def full_sum(self, unit):
        if not 0 <= unit < len(SUM_UNITS):
            return

        @pl.when(jnp.logical_not(self.is_rim))
        def _():
            self.wait(unit, 8)
            self.view(self.total, unit, "all")[...] = (
                self.view(self.half, unit, "all")[...].astype(jnp.float32)
                + self.view(self.inner, unit, "all")[...].astype(jnp.float32)
            ).astype(jnp.bfloat16)
            self.start(unit, 9)

    def finish(self):
        units = range(len(SUM_UNITS))

        @pl.when(self.is_rim)
        def _():
            for unit in units:
                self.wait(unit, 9)

        for unit in units:
            table = self.lanes(unit)
            for lane in range(1, 7):
                self.copy(unit, lane, *table[lane]).wait_send()

        @pl.when(self.is_rim)
        def _():
            for unit in units:
                self.copy(unit, 7, *self.lanes(unit)[7]).wait_send()

        @pl.when(jnp.logical_not(self.is_rim))
        def _():
            for unit in units:
                for lane in (8, 9):
                    self.copy(unit, lane, *self.lanes(unit)[lane]).wait_send()


def vector_sum(place, current, parts, send_sems, recv_sems, rim_z, core_z, is_rim):
    def copy(step, peer):
        return remote(
            current.at[step], parts.at[step], send_sems.at[step], recv_sems.at[step], peer
        )

    for step, kind in enumerate("sxy"):
        copy(step, place.peer(kind)).start()
        copy(step, place.peer(kind)).wait_recv()
        current[step + 1] = current[step] + parts[step]

    @pl.when(is_rim)
    def _():
        copy(3, (place.d, core_z)).start()

    @pl.when(jnp.logical_not(is_rim))
    def _():
        copy(3, (place.d, rim_z)).wait_recv()
        current[4] = current[3] + parts[3]
        copy(4, (place.d, 3 - place.z)).start()
        copy(4, (place.d, 3 - place.z)).wait_recv()
        current[5] = current[4] + parts[4]
        copy(5, (place.d, rim_z)).start()
        current[6] = current[5]

    @pl.when(is_rim)
    def _():
        copy(5, (place.d, core_z)).wait_recv()
        current[6] = parts[5]
        copy(3, (place.d, core_z)).wait_send()

    for step, kind in enumerate("sxy"):
        copy(step, place.peer(kind)).wait_send()

    @pl.when(jnp.logical_not(is_rim))
    def _():
        copy(4, (place.d, 3 - place.z)).wait_send()
        copy(5, (place.d, rim_z)).wait_send()


def reduce_kernel(*refs):
    grads, vectors = refs[:6], refs[6]
    totals, vector_total = refs[7:13], refs[13]
    families = [refs[14 + 6 * i : 20 + 6 * i] for i in range(8)]
    current, parts, send_sems, recv_sems, vec_send, vec_recv = refs[62:]
    place = Place()
    greet(place)
    reduce = Reduce(place, families + [totals], send_sems, recv_sems)
    for unit, (w, col, width) in enumerate(SUM_UNITS):
        reduce.sibling(unit, grads[w].at[:, 1 - place.c, :, pl.ds(col, width)]).start()
    current[0] = vectors[...]
    for unit in range(len(SUM_UNITS) + 4):
        def own(quarter):
            w, col, width = SUM_UNITS[unit]
            return grads[w][quarter, place.c, :, pl.ds(col, width)].astype(jnp.float32)

        reduce.chip_sum(unit, own)
        reduce.relay(unit - 1)
        reduce.plane_sum(unit - 2)
        reduce.half_sum(unit - 3)
        reduce.full_sum(unit - 4)
    vector_sum(
        place, current, parts, vec_send, vec_recv, reduce.rim_z, reduce.core_z, reduce.is_rim
    )
    vector_total[...] = current[6]
    for unit, (w, col, width) in enumerate(SUM_UNITS):
        reduce.sibling(unit, grads[w].at[:, 1 - place.c, :, pl.ds(col, width)]).wait_send()
    reduce.finish()


def reduce_call(grads, vectors):
    vmem = pl.BlockSpec(memory_space=pltpu.VMEM)
    units = len(SUM_UNITS)
    dma = pltpu.SemaphoreType.DMA

    def family(*lead):
        return [pltpu.VMEM((*lead, ROWS[w], COLS[w]), jnp.bfloat16) for w in range(6)]

    return pl.pallas_call(
        reduce_kernel,
        out_shape=[jax.ShapeDtypeStruct((ROWS[w], COLS[w]), jnp.bfloat16) for w in range(6)]
        + [jax.ShapeDtypeStruct((16, WIDTH), jnp.float32)],
        in_specs=[vmem] * 7,
        out_specs=[vmem] * 7,
        scratch_shapes=family(4)
        + family(4)
        + family()
        + family(2)
        + family()
        + family()
        + family()
        + family()
        + [
            pltpu.VMEM((7, 16, WIDTH), jnp.float32),
            pltpu.VMEM((6, 16, WIDTH), jnp.float32),
            dma((units, 10)),
            dma((units, 10)),
            dma((6,)),
            dma((6,)),
        ],
        compiler_params=pltpu.CompilerParams(
            collective_id=1, has_side_effects=True, vmem_limit_bytes=60 << 20
        ),
        name="reduce_gradients",
    )(*grads, vectors)


def fitted_shards(
    inputs,
    block_ids,
    query_weight,
    query_bias,
    key_weight,
    value_weight,
    value_bias,
    output_weight,
    output_bias,
    attention_gain,
    attention_shift,
    expand_weight,
    expand_bias,
    reduce_weight,
    reduce_bias,
    final_gain,
    final_shift,
    cotangent,
):
    low = jnp.bfloat16
    small = [
        query_bias,
        value_bias,
        output_bias,
        attention_gain,
        attention_shift,
        reduce_bias,
        final_gain,
        final_shift,
    ]
    packed = jnp.concatenate(small + [expand_bias, jnp.zeros((896,), low)]).reshape(16, 128)
    *full, all_vectors, blocks = gather_call(
        (key_weight, value_weight, query_weight, output_weight, expand_weight, reduce_weight),
        packed,
        inputs,
    )
    key_full, value_full, query_full, output_full, expand_full, reduce_full = (
        w.reshape(-1, w.shape[-1]) for w in full
    )
    flat = all_vectors.reshape(8, 2048).astype(jnp.float32)
    (
        query_shift,
        value_shift,
        output_shift,
        norm_gain,
        norm_shift,
        reduce_shift,
        last_gain,
        last_shift,
    ) = (flat[:, 96 * i : 96 * (i + 1)].reshape(WIDTH) for i in range(8))
    expand_shift = flat[:, 768:1152].reshape(3072)
    z = lax.axis_index("seq")
    tokens = inputs[0]
    reach = blocks.reshape(3 * TOKENS, WIDTH)
    queries = (product(tokens, query_full) + query_shift).astype(low)
    keys = product(reach, key_full).astype(low)
    values = (product(reach, value_full) + value_shift).astype(low)
    documents = block_ids[0]
    mine = documents[z]
    allowed = jnp.stack(
        [
            (z - 2 + j >= 0) & (documents[jnp.maximum(z - 2 + j, 0)] == mine)
            for j in range(3)
        ]
    )
    mask = jnp.repeat(allowed, TOKENS)[None, None, :]

    def heads(a):
        return a.reshape(a.shape[0], 12, HD)

    scores = jnp.einsum(
        "qhd,khd->hqk", heads(queries), heads(keys), preferred_element_type=jnp.float32
    )
    scores = jnp.where(mask, scores * HD ** (-0.5), MASKED)
    exponent = jnp.exp(scores - jnp.max(scores, axis=-1, keepdims=True))
    probabilities = exponent / jnp.sum(exponent, axis=-1, keepdims=True)
    probabilities_low = probabilities.astype(low)
    context = (
        jnp.einsum(
            "hqk,khd->qhd", probabilities_low, heads(values), preferred_element_type=jnp.float32
        )
        .astype(low)
        .reshape(TOKENS, WIDTH)
    )
    attended = product(context, output_full) + output_shift
    hidden, first_pull = jax.vjp(
        layer_norm, tokens.astype(jnp.float32) + attended, norm_gain, norm_shift
    )
    hidden_low = hidden.astype(low)
    expanded = product(hidden_low, expand_full) + expand_shift
    activated, gelu_pull = jax.vjp(gelu_exact, expanded)
    activated_low = activated.astype(low)
    reduced = product(activated_low, reduce_full) + reduce_shift
    final_out, final_pull = jax.vjp(
        layer_norm, hidden_low.astype(jnp.float32) + reduced, last_gain, last_shift
    )
    output = final_out.astype(low)[None]
    back_final, last_scale, last_offset = final_pull(cotangent[0].astype(jnp.float32))
    back_reduced = back_final.astype(low)
    reduce_matrix = left_transposed(activated_low, back_reduced)
    back_expanded = gelu_pull(right_transposed(back_reduced, reduce_full))[0].astype(low)
    expand_matrix = left_transposed(hidden_low, back_expanded)
    back_hidden = back_final + right_transposed(back_expanded, expand_full)
    back_attended, first_scale, first_offset = first_pull(back_hidden)
    attended_low = back_attended.astype(low)
    output_matrix = left_transposed(context, attended_low)
    back_context = right_transposed(attended_low, output_full).astype(low)
    back_weights = jnp.einsum(
        "qhd,khd->hqk", heads(back_context), heads(values), preferred_element_type=jnp.float32
    )
    inner = jnp.sum(probabilities * back_weights, axis=-1, keepdims=True)
    back_scores = (probabilities * (back_weights - inner)).astype(low)
    scale = HD ** (-0.5)
    back_query = (
        (
            jnp.einsum("hqk,khd->qhd", back_scores, heads(keys), preferred_element_type=jnp.float32)
            * scale
        )
        .astype(low)
        .reshape(TOKENS, WIDTH)
    )
    back_key = (
        (
            jnp.einsum(
                "hqk,qhd->khd", back_scores, heads(queries), preferred_element_type=jnp.float32
            )
            * scale
        )
        .astype(low)
        .reshape(3 * TOKENS, WIDTH)
    )
    back_value = (
        jnp.einsum(
            "hqk,qhd->khd",
            probabilities_low,
            heads(back_context),
            preferred_element_type=jnp.float32,
        )
        .astype(low)
        .reshape(3 * TOKENS, WIDTH)
    )
    query_matrix = left_transposed(tokens, back_query)
    key_matrix = left_transposed(reach, back_key)
    value_matrix = left_transposed(reach, back_value)
    spread = right_transposed(back_key, key_full) + right_transposed(back_value, value_full)
    spread = spread.reshape(3, TOKENS, WIDTH)
    spread_low = spread[:2].astype(low)
    one_back = lax.ppermute(spread_low[1], "seq", [(1, 0), (2, 1), (3, 2)])
    two_back = lax.ppermute(spread_low[0], "seq", [(2, 0), (3, 1)])
    input_gradient = (
        back_attended
        + right_transposed(back_query, query_full)
        + spread[2]
        + one_back.astype(jnp.float32)
        + two_back.astype(jnp.float32)
    )
    expand_vector = column_sum(back_expanded)
    vectors = jnp.stack(
        [
            column_sum(back_query),
            column_sum(back_value),
            column_sum(attended_low),
            first_scale,
            first_offset,
            column_sum(back_reduced),
            last_scale,
            last_offset,
        ]
        + [expand_vector[WIDTH * i : WIDTH * (i + 1)] for i in range(4)]
        + [jnp.zeros((WIDTH,), jnp.float32)] * 4
    )
    grads = [
        g.reshape(4, 2, ROWS[w], COLS[w]).astype(low)
        for w, g in enumerate(
            (key_matrix, value_matrix, query_matrix, output_matrix, expand_matrix, reduce_matrix)
        )
    ]
    *totals, vector_total = reduce_call(grads, vectors)
    key_sum, value_sum, query_sum, output_sum, expand_sum, reduce_sum = (
        t.astype(jnp.float32) for t in totals
    )
    d = lax.axis_index("dp")
    small_sums = lax.dynamic_slice(vector_total[:8], (0, 96 * d), (8, 96))
    expand_part = lax.dynamic_slice(vector_total[8:12].reshape(3072), (384 * d,), (384,))
    return (
        output,
        input_gradient[None],
        query_sum,
        small_sums[0],
        key_sum,
        value_sum,
        small_sums[1],
        output_sum,
        small_sums[2],
        small_sums[3],
        small_sums[4],
        expand_sum,
        expand_part,
        reduce_sum,
        small_sums[5],
        small_sums[6],
        small_sums[7],
    )


def solution(mesh):
    placed = (
        P("dp", "seq", None),
        P("dp", None),
        P("dp", None),
        P("dp"),
        P("dp", None),
        P("dp", None),
        P("dp"),
        P("dp", None),
        P("dp"),
        P("dp"),
        P("dp"),
        P("dp", None),
        P("dp"),
        P("dp", None),
        P("dp"),
        P("dp"),
        P("dp"),
        P("dp", "seq", None),
    )
    fitted = mesh.shape["dp"] == 8 and mesh.shape["seq"] == 4
    return jax.shard_map(
        fitted_shards if fitted else general_shards,
        mesh=mesh,
        in_specs=placed,
        out_specs=(
            P("dp", "seq", None),
            P("dp", "seq", None),
            P("dp", None),
            P("dp"),
            P("dp", None),
            P("dp", None),
            P("dp"),
            P("dp", None),
            P("dp"),
            P("dp"),
            P("dp"),
            P("dp", None),
            P("dp"),
            P("dp", None),
            P("dp"),
            P("dp"),
            P("dp"),
        ),
        check_vma=False,
    )
```

```python
import functools

import jax
import jax.numpy as jnp
from jax import lax
from jax.experimental import pallas as pl
from jax.experimental.pallas import tpu as pltpu
from jax.sharding import PartitionSpec as P

HD = 64
BLK = 256


EPSILON = 1e-12
MASKED = -1e30
ROW_BLOCK = 512


def as_sent(value):
    return jax.tree.map(lambda a: a.astype(jnp.bfloat16) if a.dtype == jnp.float32 else a, value)


def layer_norm(values, norm_gain, norm_shift):
    middle = jnp.mean(values, axis=-1, keepdims=True)
    centred = values - middle
    spread = jnp.mean(centred * centred, axis=-1, keepdims=True)
    return centred * lax.rsqrt(spread + EPSILON) * norm_gain + norm_shift


def gelu_exact(values):
    return jax.nn.gelu(values, approximate=False)


def product(former, latter):
    return jnp.dot(former, latter, preferred_element_type=jnp.float32)


def left_transposed(former, latter):
    return lax.dot_general(
        former, latter, (((0,), (0,)), ((), ())), preferred_element_type=jnp.float32
    )


def right_transposed(former, latter):
    return lax.dot_general(
        former, latter, (((1,), (1,)), ((), ())), preferred_element_type=jnp.float32
    )


def column_sum(values):
    return jnp.sum(values.astype(jnp.float32), axis=0)


def block_mask(allowed, row_start, row_count, key_reach):
    table_part = allowed[row_start // BLK : (row_start + row_count) // BLK, : key_reach // BLK]
    return jnp.repeat(jnp.repeat(table_part, BLK, axis=0), BLK, axis=1)


def masked_scores(queries, key_rows, allowed, row_start, row_count):
    key_reach = row_start + row_count
    scores = right_transposed(queries[row_start:key_reach], key_rows[:key_reach]) * HD ** (-0.5)
    return jnp.where(block_mask(allowed, row_start, row_count, key_reach), scores, MASKED)


def head_forward(head_item, allowed):
    queries, key_rows, value_rows = head_item
    length = queries.shape[0]
    row_count = min(ROW_BLOCK, length)
    contexts = []
    totals = []
    for row_start in range(0, length, row_count):
        scores = masked_scores(queries, key_rows, allowed, row_start, row_count)
        row_peak = jnp.max(scores, axis=-1, keepdims=True)
        exponent = jnp.exp(scores - row_peak)
        row_total = jnp.sum(exponent, axis=-1, keepdims=True)
        probabilities = (exponent / row_total).astype(jnp.bfloat16)
        contexts.append(
            product(probabilities, value_rows[: row_start + row_count]).astype(jnp.bfloat16)
        )
        totals.append(row_peak[:, 0] + jnp.log(row_total[:, 0]))
    return (jnp.concatenate(contexts, axis=0), jnp.concatenate(totals, axis=0))


def head_backward(head_item, allowed):
    queries, key_rows, value_rows, context_rows, totals = head_item
    length = queries.shape[0]
    row_count = min(ROW_BLOCK, length)
    score_scale = HD ** (-0.5)
    query_parts = []
    key_total = jnp.zeros(key_rows.shape, jnp.float32)
    value_total = jnp.zeros(value_rows.shape, jnp.float32)
    for row_start in range(0, length, row_count):
        key_reach = row_start + row_count
        scores = masked_scores(queries, key_rows, allowed, row_start, row_count)
        probabilities = jnp.exp(scores - totals[row_start:key_reach, None])
        incoming = context_rows[row_start:key_reach]
        back_weights = right_transposed(incoming, value_rows[:key_reach])
        inner_sum = jnp.sum(probabilities * back_weights, axis=-1, keepdims=True)
        back_scores = (probabilities * (back_weights - inner_sum)).astype(jnp.bfloat16)
        query_parts.append(product(back_scores, key_rows[:key_reach]) * score_scale)
        key_total = key_total.at[:key_reach].add(
            left_transposed(back_scores, queries[row_start:key_reach]) * score_scale
        )
        value_total = value_total.at[:key_reach].add(
            left_transposed(probabilities.astype(jnp.bfloat16), incoming)
        )
    back_queries = jnp.concatenate(query_parts, axis=0).astype(jnp.bfloat16)
    return (back_queries, key_total.astype(jnp.bfloat16), value_total.astype(jnp.bfloat16))


def general_shards(
    inputs,
    block_ids,
    query_weight,
    query_bias,
    key_weight,
    value_weight,
    value_bias,
    output_weight,
    output_bias,
    attention_gain,
    attention_shift,
    expand_weight,
    expand_bias,
    reduce_weight,
    reduce_bias,
    final_gain,
    final_shift,
    cotangent,
):
    tokens = inputs[0]
    documents = block_ids[0]
    block_order = jnp.arange(documents.shape[0], dtype=jnp.int32)
    allowed = (documents[:, None] == documents[None, :]) & (
        block_order[None, :] <= block_order[:, None]
    )
    (
        query_full,
        query_shift,
        key_full,
        value_full,
        value_shift,
        output_full,
        output_shift,
        norm_gain,
        norm_shift,
        expand_full,
        expand_shift,
        reduce_full,
        reduce_shift,
        last_gain,
        last_shift,
    ) = (
        lax.all_gather(query_weight, "dp", axis=0, tiled=True),
        lax.all_gather(query_bias, "dp", axis=0, tiled=True),
        lax.all_gather(key_weight, "dp", axis=0, tiled=True),
        lax.all_gather(value_weight, "dp", axis=0, tiled=True),
        lax.all_gather(value_bias, "dp", axis=0, tiled=True),
        lax.all_gather(output_weight, "dp", axis=0, tiled=True),
        lax.all_gather(output_bias, "dp", axis=0, tiled=True),
        lax.all_gather(attention_gain, "dp", axis=0, tiled=True),
        lax.all_gather(attention_shift, "dp", axis=0, tiled=True),
        lax.all_gather(expand_weight, "dp", axis=0, tiled=True),
        lax.all_gather(expand_bias, "dp", axis=0, tiled=True),
        lax.all_gather(reduce_weight, "dp", axis=0, tiled=True),
        lax.all_gather(reduce_bias, "dp", axis=0, tiled=True),
        lax.all_gather(final_gain, "dp", axis=0, tiled=True),
        lax.all_gather(final_shift, "dp", axis=0, tiled=True),
    )
    queries_token = (product(tokens, query_full) + query_shift.astype(jnp.float32)).astype(
        jnp.bfloat16
    )
    keys_token = product(tokens, key_full).astype(jnp.bfloat16)
    values_token = (product(tokens, value_full) + value_shift.astype(jnp.float32)).astype(
        jnp.bfloat16
    )
    stacked = jnp.stack([queries_token, keys_token, values_token])
    spread_heads = lax.all_to_all(stacked, "seq", split_axis=2, concat_axis=1, tiled=True)
    length = spread_heads.shape[1]
    head_count = spread_heads.shape[2] // HD
    by_head = spread_heads.reshape(3, length, head_count, HD).transpose(0, 2, 1, 3)
    contexts, totals = lax.map(
        lambda head_item: head_forward(head_item, allowed), (by_head[0], by_head[1], by_head[2])
    )
    context_rows = contexts.transpose(1, 0, 2).reshape(length, head_count * HD)
    context_token = lax.all_to_all(
        as_sent(context_rows), "seq", split_axis=0, concat_axis=1, tiled=True
    ).astype(context_rows.dtype)
    attended = product(context_token, output_full) + output_shift.astype(jnp.float32)
    first_pre = tokens.astype(jnp.float32) + attended
    hidden, first_pull = jax.vjp(
        layer_norm, first_pre, norm_gain.astype(jnp.float32), norm_shift.astype(jnp.float32)
    )
    hidden_low = hidden.astype(jnp.bfloat16)
    expanded = product(hidden_low, expand_full) + expand_shift.astype(jnp.float32)
    activated, gelu_pull = jax.vjp(gelu_exact, expanded)
    activated_low = activated.astype(jnp.bfloat16)
    reduced = product(activated_low, reduce_full) + reduce_shift.astype(jnp.float32)
    final_pre = hidden_low.astype(jnp.float32) + reduced
    final_out, final_pull = jax.vjp(
        layer_norm, final_pre, last_gain.astype(jnp.float32), last_shift.astype(jnp.float32)
    )
    output = final_out.astype(jnp.bfloat16)[None]
    query_full, key_full, value_full, output_full, expand_full, reduce_full = (
        lax.all_gather(query_weight, "dp", axis=0, tiled=True),
        lax.all_gather(key_weight, "dp", axis=0, tiled=True),
        lax.all_gather(value_weight, "dp", axis=0, tiled=True),
        lax.all_gather(output_weight, "dp", axis=0, tiled=True),
        lax.all_gather(expand_weight, "dp", axis=0, tiled=True),
        lax.all_gather(reduce_weight, "dp", axis=0, tiled=True),
    )
    back_final, last_scale, last_offset = final_pull(cotangent[0].astype(jnp.float32))
    back_reduced = back_final.astype(jnp.bfloat16)
    reduce_matrix = left_transposed(activated_low, back_reduced)
    reduce_vector = column_sum(back_reduced)
    back_activated = right_transposed(back_reduced, reduce_full)
    back_expanded = gelu_pull(back_activated)[0].astype(jnp.bfloat16)
    expand_matrix = left_transposed(hidden_low, back_expanded)
    expand_vector = column_sum(back_expanded)
    back_hidden = back_final + right_transposed(back_expanded, expand_full)
    back_attended, first_scale, first_offset = first_pull(back_hidden)
    attended_low = back_attended.astype(jnp.bfloat16)
    output_matrix = left_transposed(context_token, attended_low)
    output_vector = column_sum(attended_low)
    back_context = right_transposed(attended_low, output_full).astype(jnp.bfloat16)
    context_spread = lax.all_to_all(back_context, "seq", split_axis=1, concat_axis=0, tiled=True)
    context_by_head = context_spread.reshape(length, head_count, HD).transpose(1, 0, 2)
    back_heads = lax.map(
        lambda head_item: head_backward(head_item, allowed),
        (by_head[0], by_head[1], by_head[2], context_by_head, totals),
    )
    back_stacked = jnp.stack(back_heads).transpose(0, 2, 1, 3).reshape(3, length, head_count * HD)
    back_token = lax.all_to_all(
        as_sent(back_stacked), "seq", split_axis=1, concat_axis=2, tiled=True
    ).astype(back_stacked.dtype)
    back_query = back_token[0]
    back_key = back_token[1]
    back_value = back_token[2]
    input_gradient = (
        back_attended
        + right_transposed(back_query, query_full)
        + right_transposed(back_key, key_full)
        + right_transposed(back_value, value_full)
    )
    query_matrix = left_transposed(tokens, back_query)
    query_vector = column_sum(back_query)
    key_matrix = left_transposed(tokens, back_key)
    value_matrix = left_transposed(tokens, back_value)
    value_vector = column_sum(back_value)
    (
        query_matrix,
        query_vector,
        key_matrix,
        value_matrix,
        value_vector,
        output_matrix,
        output_vector,
        first_scale,
        first_offset,
        expand_matrix,
        expand_vector,
        reduce_matrix,
        reduce_vector,
        last_scale,
        last_offset,
    ) = (
        lax.psum_scatter(query_matrix, "dp", scatter_dimension=0, tiled=True),
        lax.psum_scatter(query_vector, "dp", scatter_dimension=0, tiled=True),
        lax.psum_scatter(key_matrix, "dp", scatter_dimension=0, tiled=True),
        lax.psum_scatter(value_matrix, "dp", scatter_dimension=0, tiled=True),
        lax.psum_scatter(value_vector, "dp", scatter_dimension=0, tiled=True),
        lax.psum_scatter(output_matrix, "dp", scatter_dimension=0, tiled=True),
        lax.psum_scatter(output_vector, "dp", scatter_dimension=0, tiled=True),
        lax.psum_scatter(first_scale, "dp", scatter_dimension=0, tiled=True),
        lax.psum_scatter(first_offset, "dp", scatter_dimension=0, tiled=True),
        lax.psum_scatter(expand_matrix, "dp", scatter_dimension=0, tiled=True),
        lax.psum_scatter(expand_vector, "dp", scatter_dimension=0, tiled=True),
        lax.psum_scatter(reduce_matrix, "dp", scatter_dimension=0, tiled=True),
        lax.psum_scatter(reduce_vector, "dp", scatter_dimension=0, tiled=True),
        lax.psum_scatter(last_scale, "dp", scatter_dimension=0, tiled=True),
        lax.psum_scatter(last_offset, "dp", scatter_dimension=0, tiled=True),
    )
    owned = (
        lax.psum(query_matrix.astype(jnp.bfloat16), "seq").astype(jnp.float32),
        lax.psum(query_vector.astype(jnp.bfloat16), "seq").astype(jnp.float32),
        lax.psum(key_matrix.astype(jnp.bfloat16), "seq").astype(jnp.float32),
        lax.psum(value_matrix.astype(jnp.bfloat16), "seq").astype(jnp.float32),
        lax.psum(value_vector.astype(jnp.bfloat16), "seq").astype(jnp.float32),
        lax.psum(output_matrix.astype(jnp.bfloat16), "seq").astype(jnp.float32),
        lax.psum(output_vector.astype(jnp.bfloat16), "seq").astype(jnp.float32),
        lax.psum(first_scale.astype(jnp.bfloat16), "seq").astype(jnp.float32),
        lax.psum(first_offset.astype(jnp.bfloat16), "seq").astype(jnp.float32),
        lax.psum(expand_matrix.astype(jnp.bfloat16), "seq").astype(jnp.float32),
        lax.psum(expand_vector.astype(jnp.bfloat16), "seq").astype(jnp.float32),
        lax.psum(reduce_matrix.astype(jnp.bfloat16), "seq").astype(jnp.float32),
        lax.psum(reduce_vector.astype(jnp.bfloat16), "seq").astype(jnp.float32),
        lax.psum(last_scale.astype(jnp.bfloat16), "seq").astype(jnp.float32),
        lax.psum(last_offset.astype(jnp.bfloat16), "seq").astype(jnp.float32),
    )
    return (output, input_gradient[None]) + tuple(owned)


MESH = pl.DeviceIdType.MESH
KEY, VALUE, QUERY, OUT, EXPAND, REDUCE = range(6)
ROWS = (96, 96, 96, 96, 96, 384)
COLS = (768, 768, 768, 768, 3072, 768)
GATHER_UNITS = (
    [(w, 0, 768, False) for w in (KEY, VALUE, QUERY, OUT)]
    + [(EXPAND, 768 * j, 768, True) for j in range(4)]
    + [(REDUCE, 256 * j, 256, True) for j in range(3)]
)
SUM_UNITS = (
    [(REDUCE, 256 * j, 256) for j in range(3)]
    + [(EXPAND, 768 * j, 768) for j in range(4)]
    + [(w, 0, 768) for w in (OUT, QUERY, KEY, VALUE)]
)
TOKENS = 256
WIDTH = 768


class Place:
    def __init__(self):
        self.d = lax.axis_index("dp")
        self.z = lax.axis_index("seq")
        self.y = self.d // 4
        self.x = (self.d // 2) % 2
        self.c = self.d % 2
        self.parity = self.z % 2
        self.partner_z = self.z + 1 - 2 * self.parity

    def shard(self, flip_y, flip_x, flip_c):
        y = 1 - self.y if flip_y else self.y
        x = 1 - self.x if flip_x else self.x
        c = 1 - self.c if flip_c else self.c
        return 4 * y + 2 * x + c

    def quarter(self, flip_y, flip_x):
        y = 1 - self.y if flip_y else self.y
        x = 1 - self.x if flip_x else self.x
        return 2 * y + x

    def peer(self, kind):
        if kind == "x":
            return (self.shard(0, 1, 0), self.z)
        if kind == "y":
            return (self.shard(1, 0, 0), self.z)
        if kind == "s":
            return (self.shard(0, 0, 1), self.z)
        return (self.d, self.partner_z)


def remote(source, target, send_sem, recv_sem, peer):
    return pltpu.make_async_remote_copy(
        src_ref=source,
        dst_ref=target,
        send_sem=send_sem,
        recv_sem=recv_sem,
        device_id=peer,
        device_id_type=MESH,
    )


class Gather:
    def __init__(self, place, own, full, send_sems, recv_sems):
        self.place, self.own, self.full = place, own, full
        self.send_sems, self.recv_sems = send_sems, recv_sems

    def rows(self, unit, part):
        w, _, _, paired = GATHER_UNITS[unit]
        count = ROWS[w]
        parity = self.place.parity
        if part == "all":
            return pl.ds(0, count)
        if not paired:
            half = count // 2
            return {"a": pl.ds(0, half), "b": pl.ds(half, half), "ab": pl.ds(0, count)}[part]
        third = count // 3
        if part == "a":
            return pl.ds(pl.multiple_of(2 * third * parity, third), third)
        if part == "b":
            return pl.ds(third, third)
        if part == "w":
            return pl.ds(pl.multiple_of(2 * third * (1 - parity), third), third)
        return pl.ds(pl.multiple_of(third * parity, third), 2 * third)

    def slot(self, unit, shard, part):
        w, col, width, _ = GATHER_UNITS[unit]
        return self.full[w].at[shard, self.rows(unit, part), pl.ds(col, width)]

    def copy(self, unit, lane, kind, shard, part, source=None):
        target = self.slot(unit, shard, part)
        return remote(
            target if source is None else source,
            target,
            self.send_sems.at[unit, lane],
            self.recv_sems.at[unit, lane],
            self.place.peer(kind),
        )

    def own_source(self, unit, part):
        w, col, width, _ = GATHER_UNITS[unit]
        return self.own[w].at[self.rows(unit, part), pl.ds(col, width)]

    def sends(self, unit):
        p = self.place
        mine, over_x, over_y, over_d = p.d, p.shard(0, 1, 0), p.shard(1, 0, 0), p.shard(1, 1, 0)
        table = {
            0: ("x", mine, "ab", True),
            1: ("x", over_y, "a", False),
            2: ("y", mine, "ab", True),
            3: ("y", over_x, "b", False),
            4: ("s", mine, "all", True),
            5: ("s", over_x, "ab", False),
            6: ("s", over_y, "ab", False),
            7: ("s", over_d, "ab", False),
        }
        if GATHER_UNITS[unit][3]:
            table.update(
                {
                    8: ("z", over_x, "a", False),
                    9: ("z", over_y, "a", False),
                    10: ("z", over_d, "a", False),
                    11: ("s", over_x, "w", False),
                    12: ("s", over_y, "w", False),
                    13: ("s", over_d, "w", False),
                }
            )
        return table

    def arrivals(self, unit):
        p = self.place
        over_x, over_y, over_d = p.shard(0, 1, 0), p.shard(1, 0, 0), p.shard(1, 1, 0)
        sib, sib_x, sib_y, sib_d = p.shard(0, 0, 1), p.shard(0, 1, 1), p.shard(1, 0, 1), p.shard(1, 1, 1)
        return {
            0: ("x", over_x, "ab"),
            1: ("x", over_d, "a"),
            2: ("y", over_y, "ab"),
            3: ("y", over_d, "b"),
            4: ("s", sib, "all"),
            5: ("s", sib_x, "ab"),
            6: ("s", sib_y, "ab"),
            7: ("s", sib_d, "ab"),
            8: ("z", over_x, "w"),
            9: ("z", over_y, "w"),
            10: ("z", over_d, "w"),
            11: ("s", sib_x, "w"),
            12: ("s", sib_y, "w"),
            13: ("s", sib_d, "w"),
        }

    def start(self, unit, *lanes):
        table = self.sends(unit)
        for lane in lanes:
            if lane in table:
                kind, shard, part, from_own = table[lane]
                source = self.own_source(unit, part) if from_own else None
                self.copy(unit, lane, kind, shard, part, source).start()

    def wait(self, unit, *lanes):
        table = self.sends(unit)
        for lane in lanes:
            if lane in table:
                kind, shard, part = self.arrivals(unit)[lane]
                self.copy(unit, lane, kind, shard, part).wait_recv()

    def open(self, unit):
        if unit < len(GATHER_UNITS):
            self.start(unit, 0, 2, 4)

    def relay(self, unit):
        if 0 <= unit < len(GATHER_UNITS):
            self.wait(unit, 0)
            self.start(unit, 3, 8, 5)
            self.wait(unit, 2)
            self.start(unit, 1, 9, 6)

    def relay_far(self, unit):
        if 0 <= unit < len(GATHER_UNITS):
            self.wait(unit, 1)
            self.start(unit, 10)
            self.wait(unit, 3)
            self.start(unit, 7)
            self.wait(unit, 8)
            self.start(unit, 11)
            self.wait(unit, 9)
            self.start(unit, 12)

    def relay_last(self, unit):
        if 0 <= unit < len(GATHER_UNITS):
            self.wait(unit, 10)
            self.start(unit, 13)

    def arrived(self, unit):
        if 0 <= unit < len(GATHER_UNITS):
            self.wait(unit, 4, 5, 6, 7, 11, 12, 13)

    def drain(self):
        for unit in range(len(GATHER_UNITS)):
            for lane, (kind, shard, part, from_own) in self.sends(unit).items():
                source = self.own_source(unit, part) if from_own else None
                self.copy(unit, lane, kind, shard, part, source).wait_send()


PLANE = [(fy, fx, fc) for fy in (0, 1) for fx in (0, 1) for fc in (0, 1)][1:]


def greet(place):
    barrier = pltpu.get_barrier_semaphore()
    for flips in PLANE:
        pl.semaphore_signal(
            barrier, inc=1, device_id=(place.shard(*flips), place.z), device_id_type=MESH
        )

    @pl.when(place.z > 0)
    def _():
        pl.semaphore_signal(barrier, inc=1, device_id=(place.d, place.z - 1), device_id_type=MESH)

    @pl.when(place.z < 3)
    def _():
        pl.semaphore_signal(barrier, inc=1, device_id=(place.d, place.z + 1), device_id_type=MESH)

    pl.semaphore_wait(barrier, 8 + (place.z * (3 - place.z)) // 2)


def cut(unit, part):
    count = ROWS[SUM_UNITS[unit][0]]
    half = count // 2
    return {"a": pl.ds(0, half), "b": pl.ds(half, half), "all": pl.ds(0, count)}[part]


class Reduce:
    def __init__(self, place, buffers, send_sems, recv_sems):
        self.place = place
        self.chip, self.far, self.near, self.outer, self.inner, self.total = buffers
        self.send_sems, self.recv_sems = send_sems, recv_sems
        self.rim_z = jnp.where(place.z < 2, 0, 3)
        self.core_z = jnp.where(place.z < 2, 1, 2)
        self.is_rim = (place.z == 0) | (place.z == 3)

    def view(self, family, unit, part, *lead):
        w, col, width = SUM_UNITS[unit]
        return family[w].at[(*lead, cut(unit, part), pl.ds(col, width))]

    def copy(self, unit, lane, source, target, peer):
        return remote(
            source, target, self.send_sems.at[unit, lane], self.recv_sems.at[unit, lane], peer
        )

    def sibling(self, unit, source):
        w, col, width = SUM_UNITS[unit]
        return self.copy(
            unit, 0, source, self.chip[w].at[:, :, pl.ds(col, width)], self.place.peer("s")
        )

    def lanes(self, unit):
        p = self.place
        to_x, to_y, to_d = p.quarter(0, 1), p.quarter(1, 0), p.quarter(1, 1)
        c, f, n = self.chip, self.far, self.near
        x, y = p.peer("x"), p.peer("y")
        return {
            1: (self.view(c, unit, "a", to_d), self.view(f, unit, "a"), x),
            2: (self.view(c, unit, "b", to_d), self.view(f, unit, "b"), y),
            3: (self.view(c, unit, "a", to_x), self.view(n, unit, "a", 0), x),
            4: (self.view(c, unit, "b", to_x), self.view(n, unit, "b", 0), x),
            5: (self.view(c, unit, "b", to_y), self.view(n, unit, "b", 1), y),
            6: (self.view(c, unit, "a", to_y), self.view(n, unit, "a", 1), y),
            7: (
                self.view(c, unit, "all", p.quarter(0, 0)),
                self.view(self.outer, unit, "all"),
                (p.d, self.core_z),
            ),
            8: (
                self.view(self.outer, unit, "all"),
                self.view(self.inner, unit, "all"),
                (p.d, 3 - self.core_z),
            ),
            9: (
                self.view(self.total, unit, "all"),
                self.view(self.total, unit, "all"),
                (p.d, self.rim_z),
            ),
        }

    def start(self, unit, *lanes):
        table = self.lanes(unit)
        for lane in lanes:
            self.copy(unit, lane, *table[lane]).start()

    def wait(self, unit, *lanes):
        table = self.lanes(unit)
        for lane in lanes:
            self.copy(unit, lane, *table[lane]).wait_recv()

    def chip_sum(self, unit, add_own):
        if not 0 <= unit < len(SUM_UNITS):
            return
        w, col, width = SUM_UNITS[unit]
        self.sibling(unit, self.chip[w].at[:, :, pl.ds(col, width)]).wait_recv()
        add_own()
        self.start(unit, 1, 2, 3, 5)

    def relay(self, unit):
        if not 0 <= unit < len(SUM_UNITS):
            return
        p = self.place
        for lane, part, quarter, after in (
            (1, "a", p.quarter(1, 0), 6),
            (2, "b", p.quarter(0, 1), 4),
        ):
            self.wait(unit, lane)
            target = self.view(self.chip, unit, part, quarter)
            target[...] = (
                target[...].astype(jnp.float32)
                + self.view(self.far, unit, part)[...].astype(jnp.float32)
            ).astype(jnp.bfloat16)
            self.start(unit, after)

    def plane_sum(self, unit):
        if not 0 <= unit < len(SUM_UNITS):
            return
        mine = self.place.quarter(0, 0)
        self.wait(unit, 3, 4, 5, 6)
        total = self.view(self.chip, unit, "all", mine)[...].astype(jnp.float32)
        for side in (0, 1):
            total = total + self.view(self.near, unit, "all", side)[...].astype(jnp.float32)
        self.view(self.chip, unit, "all", mine)[...] = total.astype(jnp.bfloat16)

        @pl.when(self.is_rim)
        def _():
            self.start(unit, 7)

    def half_sum(self, unit):
        if not 0 <= unit < len(SUM_UNITS):
            return

        @pl.when(jnp.logical_not(self.is_rim))
        def _():
            self.wait(unit, 7)
            self.view(self.outer, unit, "all")[...] = (
                self.view(self.chip, unit, "all", self.place.quarter(0, 0))[...].astype(jnp.float32)
                + self.view(self.outer, unit, "all")[...].astype(jnp.float32)
            ).astype(jnp.bfloat16)
            self.start(unit, 8)

    def full_sum(self, unit):
        if not 0 <= unit < len(SUM_UNITS):
            return

        @pl.when(jnp.logical_not(self.is_rim))
        def _():
            self.wait(unit, 8)
            self.view(self.total, unit, "all")[...] = (
                self.view(self.outer, unit, "all")[...].astype(jnp.float32)
                + self.view(self.inner, unit, "all")[...].astype(jnp.float32)
            ).astype(jnp.bfloat16)
            self.start(unit, 9)

    def finish(self):
        units = range(len(SUM_UNITS))

        @pl.when(self.is_rim)
        def _():
            for unit in units:
                self.wait(unit, 9)

        for unit in units:
            table = self.lanes(unit)
            for lane in range(1, 7):
                self.copy(unit, lane, *table[lane]).wait_send()

        @pl.when(self.is_rim)
        def _():
            for unit in units:
                self.copy(unit, 7, *self.lanes(unit)[7]).wait_send()

        @pl.when(jnp.logical_not(self.is_rim))
        def _():
            for unit in units:
                for lane in (8, 9):
                    self.copy(unit, lane, *self.lanes(unit)[lane]).wait_send()


class VectorSum:
    def __init__(self, place, reduce, current, parts, send_sems, recv_sems):
        self.current, self.parts = current, parts
        self.send_sems, self.recv_sems = send_sems, recv_sems
        self.is_rim = reduce.is_rim
        self.is_core = jnp.logical_not(reduce.is_rim)
        self.peers = [place.peer(kind) for kind in "sxy"] + [
            (place.d, reduce.core_z),
            (place.d, 3 - place.z),
            (place.d, reduce.rim_z),
        ]

    def copy(self, step):
        return remote(
            self.current.at[step],
            self.parts.at[step],
            self.send_sems.at[step],
            self.recv_sems.at[step],
            self.peers[step],
        )

    def take(self, step):
        self.copy(step).wait_recv()
        self.current[step + 1] = self.current[step] + self.parts[step]

    def phase(self, number):
        if number == 0:
            self.copy(0).start()
        elif number < 3:
            self.take(number - 1)
            self.copy(number).start()
        elif number == 3:
            self.take(2)

            @pl.when(self.is_rim)
            def _():
                self.copy(3).start()

        elif number in (4, 5):

            @pl.when(self.is_core)
            def _():
                self.take(number - 1)
                self.copy(number).start()
                if number == 5:
                    self.current[6] = self.current[5]

        else:

            @pl.when(self.is_rim)
            def _():
                self.copy(5).wait_recv()
                self.current[6] = self.parts[5]
                self.copy(3).wait_send()

            for step in range(3):
                self.copy(step).wait_send()

            @pl.when(self.is_core)
            def _():
                self.copy(4).wait_send()
                self.copy(5).wait_send()


def chunk(index, size):
    return pl.ds(pl.multiple_of(index * size, size), size)


def loop(count, body):
    def step(index, carry):
        body(index)
        return carry

    lax.fori_loop(0, count, step, 0)


def fold_rows(values):
    return values[0:8] + values[8:16] + values[16:24] + values[24:32]


def layer_kernel(*refs):
    own = refs[:6]
    vectors, tokens, cotangent, block_ids = refs[6:10]
    output, gradient = refs[10:12]
    totals, vector_total = refs[12:18], refs[18]
    refs = refs[19:]
    full, refs = refs[:6], refs[6:]
    families = [refs[6 * i : 6 * (i + 1)] for i in range(5)]
    refs = refs[30:]
    (
        ring_reduce,
        ring_other,
        all_vectors,
        vecs,
        expand_shift,
        blocks,
        tangent,
        reach_t,
        queries,
        keys,
        values,
        keys_t,
        values_t,
        weights_t,
        context_t,
        context,
        first_norm,
        first_rate,
        hidden,
        hidden_t,
        active,
        active_t,
        slope,
        back_reduced,
        attended_low,
        back_context,
        back_query_t,
        back_query,
        back_key,
        spread_send,
        spread_recv,
        sums,
        expand_sum,
        current,
        parts,
    ) = refs[:35]
    (
        local_sems,
        gather_send,
        gather_recv,
        vec_send,
        vec_recv,
        tok_send,
        tok_recv,
        sum_send,
        sum_recv,
        small_send,
        small_recv,
        spread_ssem,
        spread_rsem,
    ) = refs[35:]
    back_expanded = active
    back_value = values_t
    f32, low = jnp.float32, jnp.bfloat16
    place = Place()
    gather = Gather(place, own, full, gather_send, gather_recv)
    reduce = Reduce(place, families + [totals], sum_send, sum_recv)
    small = VectorSum(place, reduce, current, parts, small_send, small_recv)
    local = [pltpu.make_async_copy(own[w], full[w].at[place.d], local_sems.at[w]) for w in range(6)]
    local.append(pltpu.make_async_copy(vectors, all_vectors.at[place.d], local_sems.at[6]))
    local.append(pltpu.make_async_copy(tokens.at[0], blocks.at[2], local_sems.at[7]))
    local.append(pltpu.make_async_copy(cotangent.at[0], tangent, local_sems.at[8]))
    for copy in local:
        copy.start()
    greet(place)

    def tick(unit):
        gather.relay(unit)
        gather.open(unit + 3)
        gather.relay_far(unit - 1)
        gather.relay_last(unit - 2)

    def vector_copy(i, shard, peer):
        return remote(vectors, all_vectors.at[shard], vec_send.at[i], vec_recv.at[i], peer)

    def token_copy(slot, source, peer_z):
        return remote(
            source, blocks.at[slot], tok_send.at[slot], tok_recv.at[slot], (place.d, peer_z)
        )

    for i, flips in enumerate(PLANE):
        vector_copy(i, place.d, (place.shard(*flips), place.z)).start()

    @pl.when(place.z < 3)
    def _():
        token_copy(1, tokens.at[0], place.z + 1).start()

    for unit in range(3):
        gather.open(unit)

    @pl.when(place.z == 0)
    def _():
        blocks[0] = jnp.zeros((TOKENS, WIDTH), low)
        blocks[1] = jnp.zeros((TOKENS, WIDTH), low)

    @pl.when(place.z == 1)
    def _():
        blocks[0] = jnp.zeros((TOKENS, WIDTH), low)

    for copy in local:
        copy.wait()

    def turn(slot):
        reach_t[:, slot * TOKENS : (slot + 1) * TOKENS] = blocks[slot].T

    turn(2)
    sums[...] = jnp.zeros_like(sums)
    tick(0)

    @pl.when(place.z > 0)
    def _():
        token_copy(1, tokens.at[0], place.z - 1).wait_recv()

        @pl.when(place.z < 3)
        def _():
            token_copy(0, blocks.at[1], place.z + 1).start()

    turn(1)
    for i, flips in enumerate(PLANE):
        vector_copy(i, place.shard(*flips), (place.shard(*flips), place.z)).wait_recv()

    def place_vectors(s, total):
        row = lax.broadcasted_iota(jnp.int32, (128, WIDTH), 0)
        lane = lax.broadcasted_iota(jnp.int32, (128, WIDTH), 1)
        pick = jnp.where((lane == row + 96 * s) & (row < 96), 1.0, 0.0).astype(low)
        return total + product(all_vectors[s], pick)

    vecs[...] = lax.fori_loop(0, 8, place_vectors, jnp.zeros((16, WIDTH), f32))
    for s in range(8):
        rows = all_vectors[s].astype(f32)
        for r in range(3):
            expand_shift[:, 384 * s + 128 * r : 384 * s + 128 * (r + 1)] = rows[8 + r : 9 + r, :]
    tick(1)

    def weight_columns(w, cols):
        return full[w][:, :, cols].reshape(8 * ROWS[w], 256)

    def project_keys(first, count):
        def body(i):
            cols = chunk(i, 256)
            source = blocks[first : first + count].reshape(count * TOKENS, WIDTH)
            part = product(source, weight_columns(KEY, cols)).astype(low)
            toks = slice(first * TOKENS, (first + count) * TOKENS)
            keys[toks, cols] = part
            keys_t[cols, toks] = part.T

        loop(3, body)

    def project_values(first, count):
        def body(i):
            cols = chunk(i, 256)
            source = blocks[first : first + count].reshape(count * TOKENS, WIDTH)
            part = (product(source, weight_columns(VALUE, cols)) + vecs[1:2, cols]).astype(low)
            toks = slice(first * TOKENS, (first + count) * TOKENS)
            values[toks, cols] = part
            values_t[cols, toks] = part.T

        loop(3, body)

    gather.arrived(0)
    project_keys(1, 2)
    tick(2)
    gather.arrived(1)
    project_values(1, 2)

    @pl.when(place.z > 1)
    def _():
        token_copy(0, blocks.at[1], place.z - 1).wait_recv()

    tick(3)
    turn(0)
    project_keys(0, 1)
    project_values(0, 1)
    gather.arrived(2)

    def project_queries(i):
        cols = chunk(i, 256)
        part = (product(blocks[2], weight_columns(QUERY, cols)) + vecs[0:1, cols]).astype(low)
        queries[:, cols] = (part.astype(f32) * HD ** (-0.5)).astype(low)

    loop(3, project_queries)

    mine = block_ids[0, place.z]
    biases = []
    for slot in range(2):
        source = place.z - 2 + slot
        seen = (source >= 0) & (block_ids[0, jnp.maximum(source, 0)] == mine)
        biases.append(jnp.where(seen, 0.0, MASKED).astype(f32))

    def half_lanes(values, half):
        lane = lax.broadcasted_iota(jnp.int32, values.shape, 1)
        keep = (lane >= 64) if half else (lane < 64)
        return jnp.where(keep, values, jnp.zeros_like(values))

    def attend(first, count):
        def body(i):
            pair = first + i
            cols = chunk(pair, 128)
            pair_queries = queries[:, cols]
            for half in range(2):
                masked = half_lanes(pair_queries, half)
                scores = [
                    right_transposed(keys[slot * TOKENS : (slot + 1) * TOKENS, cols], masked)
                    for slot in range(3)
                ]
                scores = [scores[0] + biases[0], scores[1] + biases[1], scores[2]]
                peak = jnp.maximum(
                    jnp.maximum(
                        jnp.max(scores[0], axis=0, keepdims=True),
                        jnp.max(scores[1], axis=0, keepdims=True),
                    ),
                    jnp.max(scores[2], axis=0, keepdims=True),
                )
                powers = [jnp.exp(s - peak) for s in scores]
                total = sum(jnp.sum(p, axis=0, keepdims=True) for p in powers)
                share = 1.0 / total
                for slot in range(3):
                    weights_t[2 * pair + half, slot * TOKENS : (slot + 1) * TOKENS, :] = (
                        powers[slot] * share
                    ).astype(low)
                rows = pl.ds(pl.multiple_of(pair * 128 + half * 64, 64), 64)
                context_t[rows, :] = product(values_t[rows, :], weights_t[2 * pair + half]).astype(
                    low
                )

        loop(count, body)

    attend(0, 2)
    tick(4)
    attend(2, 2)
    tick(5)
    attend(4, 2)
    gather.arrived(3)

    def project_output(i):
        cols = chunk(i, 256)
        if True:
            part = product(context[...], weight_columns(OUT, cols)) + vecs[2:3, cols]
        gradient[:, cols] = part + blocks[2, :, cols].astype(f32)

    context[...] = context_t[...].T
    loop(3, project_output)

    def mean(values):
        return jnp.sum(values, axis=-1, keepdims=True) * (1.0 / WIDTH)

    def first_normalise(i):
        rows = chunk(i, 32)
        values = gradient[rows, :]
        centred = values - mean(values)
        rate = lax.rsqrt(mean(centred * centred) + EPSILON)
        norm = centred * rate
        first_norm[rows, :] = norm
        first_rate[rows, :] = jnp.broadcast_to(rate, (32, 128))
        hidden[rows, :] = (norm * vecs[3:4, :] + vecs[4:5, :]).astype(low)

    loop(8, first_normalise)
    hidden_t[...] = hidden[...].T
    tick(6)

    def expand(unit):
        def body(i):
            cols = chunk(3 * unit + i, 256)
            inner = product(hidden[...], weight_columns(EXPAND, cols)) + expand_shift[:, cols]
            share = 0.5 * (1.0 + lax.erf(inner * 0.7071067811865476))
            bell = jnp.exp(inner * inner * -0.5) * 0.3989422804014327
            act = (inner * share).astype(low)
            active[:, cols] = act
            active_t[cols, :] = act.T
            slope[:, cols] = (share + inner * bell).astype(low)

        loop(3, body)

    for j in range(4):
        gather.arrived(4 + j)
        expand(j)
        tick(7 + j)

    for j in range(3):
        if j:
            tick(10 + j)
        gather.arrived(8 + j)
        cols = slice(256 * j, 256 * (j + 1))
        part = product(active[...], full[REDUCE][:, :, cols].reshape(3072, 256))
        gradient[:, cols] = part + vecs[5:6, cols] + hidden[:, cols].astype(f32)

    def last_normalise(i):
        rows = chunk(i, 32)
        values = gradient[rows, :]
        centred = values - mean(values)
        rate = lax.rsqrt(mean(centred * centred) + EPSILON)
        norm = centred * rate
        output[rows, :] = (norm * vecs[6:7, :] + vecs[7:8, :]).astype(low)
        arriving = tangent[rows, :].astype(f32)
        sums[0] += fold_rows(arriving * norm)
        sums[1] += fold_rows(arriving)
        scaled = arriving * vecs[6:7, :]
        back = (scaled - mean(scaled) - norm * mean(scaled * norm)) * rate
        gradient[rows, :] = back
        rounded = back.astype(low)
        back_reduced[rows, :] = rounded
        sums[2] += fold_rows(rounded.astype(f32))

    loop(8, last_normalise)

    def shard_rows(shard, count):
        return pl.ds(pl.multiple_of(shard * count, 32), count)

    def group(source, parity, toks=None):
        picks = []
        for quarter in range(4):
            rows = shard_rows(2 * quarter + parity, 96)
            picks.append(source[rows, :] if toks is None else source[rows, toks])
        return jnp.concatenate(picks, axis=0)

    def terms(unit, parity, put):
        w, col, width = SUM_UNITS[unit]
        if w == REDUCE:

            def body(quarter):
                rows = shard_rows(2 * quarter + parity, 384)
                put(
                    quarter,
                    slice(0, 256),
                    product(active_t[rows, :], back_reduced[:, col : col + 256]),
                )

            loop(4, body)
            return

        if w == EXPAND:
            lhs = lambda: group(hidden_t, parity)
            rhs = lambda i: back_expanded[:, chunk(col // 256 + i, 256)]
        elif w == OUT:
            lhs = lambda: group(context_t, parity)
            rhs = lambda i: attended_low[:, chunk(i, 256)]
        elif w == QUERY:
            lhs = lambda: group(reach_t, parity, slice(512, 768))
            rhs = lambda i: back_query[:, chunk(i, 256)]
        elif w == KEY:
            lhs = lambda: group(reach_t, parity)
            rhs = lambda i: back_key[:, chunk(i, 256)]
        else:
            lhs = lambda: group(reach_t, parity)
            rhs = lambda i: back_value[:, chunk(i, 256)]

        def body(i):
            term = product(lhs(), rhs(i))
            for quarter in range(4):
                put(quarter, chunk(i, 256), term[96 * quarter : 96 * (quarter + 1)])

        loop(3, body)

    def slot_of(unit):
        return ring_reduce.at[unit % 2] if unit < 3 else ring_other.at[(unit - 3) % 3]

    def ring_before(unit):
        return unit - 2 if unit == 2 else (unit - 3 if unit >= 6 else None)

    def send_half(unit):
        if unit >= len(SUM_UNITS):
            return
        slot = slot_of(unit)
        earlier = ring_before(unit)
        if earlier is not None:
            reduce.sibling(earlier, slot).wait_send()

        def put(quarter, cols, term):
            slot[quarter, :, cols] = term.astype(low)

        terms(unit, 1 - place.c, put)
        reduce.sibling(unit, slot).start()

    def own_half(unit):
        if unit >= len(SUM_UNITS):
            return
        w, col, width = SUM_UNITS[unit]

        def add_own():
            def put(quarter, cols, term):
                if w == REDUCE:
                    where = (quarter, slice(None), slice(col, col + 256))
                elif w == EXPAND:
                    where = (quarter, slice(None), pl.ds(pl.multiple_of(cols.start + col, 256), 256))
                else:
                    where = (quarter, slice(None), cols)
                reduce.chip[w][where] = (term + reduce.chip[w][where].astype(f32)).astype(low)

            terms(unit, place.c, put)

        reduce.chip_sum(unit, add_own)

    def step(unit):
        own_half(unit)
        reduce.relay(unit - 1)
        reduce.plane_sum(unit - 2)
        reduce.half_sum(unit - 3)
        reduce.full_sum(unit - 4)

    def back_expand(j):
        def body(i):
            shard = 2 * j + i
            cols = pl.ds(pl.multiple_of(shard * 384, 128), 384)
            back = right_transposed(back_reduced[...], full[REDUCE][shard])
            rounded = (back * slope[:, cols].astype(f32)).astype(low)
            back_expanded[:, cols] = rounded
            expand_sum[:, cols] = jnp.sum(rounded.astype(f32), axis=0, keepdims=True)

        loop(2, body)

        def gather_hidden(i):
            cols = slice(768 * j, 768 * (j + 1))
            rows = full[EXPAND][pl.ds(4 * i, 4), :, cols].reshape(384, 768)
            out = pl.ds(pl.multiple_of(i * 384, 128), 384)
            gradient[:, out] += right_transposed(back_expanded[:, cols], rows)

        loop(2, gather_hidden)

    send_half(0)
    send_half(1)
    step(0)
    back_expand(0)
    send_half(2)
    step(1)
    back_expand(1)
    send_half(3)
    step(2)
    back_expand(2)
    send_half(4)
    step(3)
    back_expand(3)
    send_half(5)
    step(4)

    def first_back(i):
        rows = chunk(i, 32)
        back = gradient[rows, :]
        norm = first_norm[rows, :]
        sums[3] += fold_rows(back * norm)
        sums[4] += fold_rows(back)
        scaled = back * vecs[3:4, :]
        rate = first_rate[rows, 0:1]
        back = (scaled - mean(scaled) - norm * mean(scaled * norm)) * rate
        gradient[rows, :] = back
        rounded = back.astype(low)
        attended_low[rows, :] = rounded
        sums[5] += fold_rows(rounded.astype(f32))

    loop(8, first_back)

    def weight_rows(w, i):
        return full[w][pl.ds(4 * i, 4), :, :].reshape(384, WIDTH)

    def back_output(i):
        out = pl.ds(pl.multiple_of(i * 384, 128), 384)
        back_context[:, out] = right_transposed(attended_low[...], weight_rows(OUT, i)).astype(low)

    loop(2, back_output)
    send_half(6)
    step(5)

    def attend_back(first, count):
        def body(i):
            pair = first + i
            cols = chunk(pair, 128)
            pair_back = back_context[:, cols]
            pair_queries = queries[:, cols]
            key_term, value_term = 0.0, 0.0
            for half in range(2):
                masked = half_lanes(pair_back, half)
                weights = weights_t[2 * pair + half].astype(f32)
                back = right_transposed(values[:, cols], masked)
                inner = jnp.sum(weights * back, axis=0, keepdims=True)
                back_scores = (weights * (back - inner)).astype(low)
                key_term += product(back_scores, half_lanes(pair_queries, half))
                value_term += product(weights_t[2 * pair + half], masked)
                rows = pl.ds(pl.multiple_of(pair * 128 + half * 64, 64), 64)
                back_query_t[rows, :] = (
                    product(keys_t[rows, :], back_scores) * HD ** (-0.5)
                ).astype(low)
            back_key[:, cols] = key_term.astype(low)
            back_value[:, cols] = value_term.astype(low)

        loop(count, body)

    attend_back(0, 3)
    send_half(7)
    step(6)
    attend_back(3, 3)
    back_query[...] = back_query_t[...].T
    send_half(8)
    step(7)

    def spread_copy(slot):
        return remote(
            spread_send.at[slot],
            spread_recv.at[slot],
            spread_ssem.at[slot],
            spread_rsem.at[slot],
            (place.d, place.z - 1),
        )

    def spread_into(block):
        toks = slice(block * TOKENS, (block + 1) * TOKENS)

        def body(i):
            out = pl.ds(pl.multiple_of(i * 384, 128), 384)
            part = right_transposed(back_key[toks, :], weight_rows(KEY, i)) + right_transposed(
                back_value[toks, :], weight_rows(VALUE, i)
            )
            if block == 2:
                part = part + right_transposed(back_query[...], weight_rows(QUERY, i))
                gradient[:, out] += part
            else:
                spread_send[block, :, out] = part.astype(low)

        loop(2, body)

    spread_into(0)

    @pl.when(place.z > 1)
    def _():
        spread_copy(0).start()

    spread_into(1)

    @pl.when(place.z == 3)
    def _():
        spread_copy(1).start()

    def column_total(values):
        return jnp.sum(values, axis=0, keepdims=True)

    rows = [
        column_total(back_query[...].astype(f32)),
        column_total(back_value[...].astype(f32)),
        column_total(sums[5]),
        column_total(sums[3]),
        column_total(sums[4]),
        column_total(sums[2]),
        column_total(sums[0]),
        column_total(sums[1]),
    ] + [expand_sum[:, WIDTH * i : WIDTH * (i + 1)] for i in range(4)]
    for i, row in enumerate(rows):
        current[0, i : i + 1, :] = row
    current[0, 12:16, :] = jnp.zeros((4, WIDTH), f32)
    small.phase(0)
    send_half(9)
    step(8)
    small.phase(1)

    @pl.when((place.z > 0) & (place.z < 3))
    def _():
        pltpu_copy = remote(
            spread_send.at[0],
            spread_recv.at[0],
            spread_ssem.at[0],
            spread_rsem.at[0],
            (place.d, place.z + 1),
        )
        pltpu_copy.wait_recv()
        spread_send[1] = (spread_send[1].astype(f32) + spread_recv[0].astype(f32)).astype(low)
        spread_copy(1).start()

    spread_into(2)
    send_half(10)
    step(9)
    small.phase(2)
    step(10)
    small.phase(3)
    step(11)
    small.phase(4)
    step(12)
    small.phase(5)
    step(13)

    @pl.when(place.z < 3)
    def _():
        remote(
            spread_send.at[1],
            spread_recv.at[1],
            spread_ssem.at[1],
            spread_rsem.at[1],
            (place.d, place.z + 1),
        ).wait_recv()

        def body(i):
            rows = chunk(i, 32)
            gradient[rows, :] += spread_recv[1, rows, :].astype(f32)

        loop(8, body)

    step(14)
    small.phase(6)
    vector_total[...] = current[6]

    gather.drain()
    for i, flips in enumerate(PLANE):
        vector_copy(i, place.d, (place.shard(*flips), place.z)).wait_send()

    @pl.when(place.z < 3)
    def _():
        token_copy(1, tokens.at[0], place.z + 1).wait_send()

    @pl.when((place.z > 0) & (place.z < 3))
    def _():
        token_copy(0, blocks.at[1], place.z + 1).wait_send()

    @pl.when(place.z > 1)
    def _():
        spread_copy(0).wait_send()

    @pl.when(place.z > 0)
    def _():
        spread_copy(1).wait_send()

    waited = [ring_before(unit) for unit in range(len(SUM_UNITS))]
    for unit in range(len(SUM_UNITS)):
        if unit not in waited:
            reduce.sibling(unit, slot_of(unit)).wait_send()
    reduce.finish()


def layer_call(weights, vectors, tokens, cotangent, block_ids):
    hbm = pl.BlockSpec(memory_space=pl.ANY)
    vmem = pl.BlockSpec(memory_space=pltpu.VMEM)
    dma = pltpu.SemaphoreType.DMA
    low, f32 = jnp.bfloat16, jnp.float32
    gathers, units = len(GATHER_UNITS), len(SUM_UNITS)

    def family(*lead):
        return [pltpu.VMEM((*lead, ROWS[w], COLS[w]), low) for w in range(6)]

    def wide(rows, cols, kind=low):
        return pltpu.VMEM((rows, cols), kind)

    scratch = (
        family(8)
        + family(4)
        + family()
        + family(2)
        + family()
        + family()
        + [
            pltpu.VMEM((2, 4, 384, 256), low),
            pltpu.VMEM((3, 4, 96, WIDTH), low),
            pltpu.VMEM((8, 16, 128), low),
            wide(16, WIDTH, f32),
            wide(1, 3072, f32),
            pltpu.VMEM((3, TOKENS, WIDTH), low),
            wide(TOKENS, WIDTH),
            wide(WIDTH, 3 * TOKENS),
            wide(TOKENS, WIDTH),
            wide(3 * TOKENS, WIDTH),
            wide(3 * TOKENS, WIDTH),
            wide(WIDTH, 3 * TOKENS),
            wide(WIDTH, 3 * TOKENS),
            pltpu.VMEM((12, 3 * TOKENS, TOKENS), low),
            wide(WIDTH, TOKENS),
            wide(TOKENS, WIDTH),
            wide(TOKENS, WIDTH, f32),
            wide(TOKENS, 128, f32),
            wide(TOKENS, WIDTH),
            wide(WIDTH, TOKENS),
            wide(TOKENS, 3072),
            wide(3072, TOKENS),
            wide(TOKENS, 3072),
            wide(TOKENS, WIDTH),
            wide(TOKENS, WIDTH),
            wide(TOKENS, WIDTH),
            wide(WIDTH, TOKENS),
            wide(TOKENS, WIDTH),
            wide(3 * TOKENS, WIDTH),
            pltpu.VMEM((2, TOKENS, WIDTH), low),
            pltpu.VMEM((2, TOKENS, WIDTH), low),
            pltpu.VMEM((6, 8, WIDTH), f32),
            wide(1, 3072, f32),
            pltpu.VMEM((7, 16, WIDTH), f32),
            pltpu.VMEM((6, 16, WIDTH), f32),
            dma((9,)),
            dma((gathers, 14)),
            dma((gathers, 14)),
            dma((7,)),
            dma((7,)),
            dma((2,)),
            dma((2,)),
            dma((units, 10)),
            dma((units, 10)),
            dma((6,)),
            dma((6,)),
            dma((2,)),
            dma((2,)),
        ]
    )
    return pl.pallas_call(
        layer_kernel,
        out_shape=[
            jax.ShapeDtypeStruct((TOKENS, WIDTH), low),
            jax.ShapeDtypeStruct((TOKENS, WIDTH), f32),
        ]
        + [jax.ShapeDtypeStruct((ROWS[w], COLS[w]), low) for w in range(6)]
        + [jax.ShapeDtypeStruct((16, WIDTH), f32)],
        in_specs=[hbm] * 9 + [pl.BlockSpec(memory_space=pltpu.SMEM)],
        out_specs=[vmem] * 9,
        scratch_shapes=scratch,
        compiler_params=pltpu.CompilerParams(
            collective_id=0, has_side_effects=True, vmem_limit_bytes=67043328
        ),
        name="layer",
    )(*weights, vectors, tokens, cotangent, block_ids)


def fitted_shards(
    inputs,
    block_ids,
    query_weight,
    query_bias,
    key_weight,
    value_weight,
    value_bias,
    output_weight,
    output_bias,
    attention_gain,
    attention_shift,
    expand_weight,
    expand_bias,
    reduce_weight,
    reduce_bias,
    final_gain,
    final_shift,
    cotangent,
):
    low = jnp.bfloat16
    small = [
        query_bias,
        value_bias,
        output_bias,
        attention_gain,
        attention_shift,
        reduce_bias,
        final_gain,
        final_shift,
    ]
    packed = jnp.concatenate(
        [
            jnp.pad(jnp.stack(small), ((0, 0), (0, 32))),
            expand_bias.reshape(3, 128),
            jnp.zeros((5, 128), low),
        ]
    )
    output, gradient, *totals, vector_total = layer_call(
        (key_weight, value_weight, query_weight, output_weight, expand_weight, reduce_weight),
        packed,
        inputs,
        cotangent,
        block_ids,
    )
    key_sum, value_sum, query_sum, output_sum, expand_sum, reduce_sum = (
        t.astype(jnp.float32) for t in totals
    )
    d = lax.axis_index("dp")
    small_sums = lax.dynamic_slice(vector_total[:8], (0, 96 * d), (8, 96))
    expand_part = lax.dynamic_slice(vector_total[8:12].reshape(3072), (384 * d,), (384,))
    return (
        output[None],
        gradient[None],
        query_sum,
        small_sums[0],
        key_sum,
        value_sum,
        small_sums[1],
        output_sum,
        small_sums[2],
        small_sums[3],
        small_sums[4],
        expand_sum,
        expand_part,
        reduce_sum,
        small_sums[5],
        small_sums[6],
        small_sums[7],
    )


def solution(mesh):
    placed = (
        P("dp", "seq", None),
        P("dp", None),
        P("dp", None),
        P("dp"),
        P("dp", None),
        P("dp", None),
        P("dp"),
        P("dp", None),
        P("dp"),
        P("dp"),
        P("dp"),
        P("dp", None),
        P("dp"),
        P("dp", None),
        P("dp"),
        P("dp"),
        P("dp"),
        P("dp", "seq", None),
    )
    fitted = mesh.shape["dp"] == 8 and mesh.shape["seq"] == 4
    return jax.shard_map(
        fitted_shards if fitted else general_shards,
        mesh=mesh,
        in_specs=placed,
        out_specs=(
            P("dp", "seq", None),
            P("dp", "seq", None),
            P("dp", None),
            P("dp"),
            P("dp", None),
            P("dp", None),
            P("dp"),
            P("dp", None),
            P("dp"),
            P("dp"),
            P("dp"),
            P("dp", None),
            P("dp"),
            P("dp", None),
            P("dp"),
            P("dp"),
            P("dp"),
        ),
        check_vma=False,
    )
```

```python
import functools

import jax
import jax.numpy as jnp
from jax import lax
from jax.experimental import pallas as pl
from jax.experimental.pallas import tpu as pltpu
from jax.sharding import PartitionSpec as P

HD = 64
BLK = 256


EPSILON = 1e-12
MASKED = -1e30
ROW_BLOCK = 512


def as_sent(value):
    return jax.tree.map(lambda a: a.astype(jnp.bfloat16) if a.dtype == jnp.float32 else a, value)


def layer_norm(values, norm_gain, norm_shift):
    middle = jnp.mean(values, axis=-1, keepdims=True)
    centred = values - middle
    spread = jnp.mean(centred * centred, axis=-1, keepdims=True)
    return centred * lax.rsqrt(spread + EPSILON) * norm_gain + norm_shift


def gelu_exact(values):
    return jax.nn.gelu(values, approximate=False)


def product(former, latter):
    return jnp.dot(former, latter, preferred_element_type=jnp.float32)


def left_transposed(former, latter):
    return lax.dot_general(
        former, latter, (((0,), (0,)), ((), ())), preferred_element_type=jnp.float32
    )


def right_transposed(former, latter):
    return lax.dot_general(
        former, latter, (((1,), (1,)), ((), ())), preferred_element_type=jnp.float32
    )


def column_sum(values):
    return jnp.sum(values.astype(jnp.float32), axis=0)


def block_mask(allowed, row_start, row_count, key_reach):
    table_part = allowed[row_start // BLK : (row_start + row_count) // BLK, : key_reach // BLK]
    return jnp.repeat(jnp.repeat(table_part, BLK, axis=0), BLK, axis=1)


def masked_scores(queries, key_rows, allowed, row_start, row_count):
    key_reach = row_start + row_count
    scores = right_transposed(queries[row_start:key_reach], key_rows[:key_reach]) * HD ** (-0.5)
    return jnp.where(block_mask(allowed, row_start, row_count, key_reach), scores, MASKED)


def head_forward(head_item, allowed):
    queries, key_rows, value_rows = head_item
    length = queries.shape[0]
    row_count = min(ROW_BLOCK, length)
    contexts = []
    totals = []
    for row_start in range(0, length, row_count):
        scores = masked_scores(queries, key_rows, allowed, row_start, row_count)
        row_peak = jnp.max(scores, axis=-1, keepdims=True)
        exponent = jnp.exp(scores - row_peak)
        row_total = jnp.sum(exponent, axis=-1, keepdims=True)
        probabilities = (exponent / row_total).astype(jnp.bfloat16)
        contexts.append(
            product(probabilities, value_rows[: row_start + row_count]).astype(jnp.bfloat16)
        )
        totals.append(row_peak[:, 0] + jnp.log(row_total[:, 0]))
    return (jnp.concatenate(contexts, axis=0), jnp.concatenate(totals, axis=0))


def head_backward(head_item, allowed):
    queries, key_rows, value_rows, context_rows, totals = head_item
    length = queries.shape[0]
    row_count = min(ROW_BLOCK, length)
    score_scale = HD ** (-0.5)
    query_parts = []
    key_total = jnp.zeros(key_rows.shape, jnp.float32)
    value_total = jnp.zeros(value_rows.shape, jnp.float32)
    for row_start in range(0, length, row_count):
        key_reach = row_start + row_count
        scores = masked_scores(queries, key_rows, allowed, row_start, row_count)
        probabilities = jnp.exp(scores - totals[row_start:key_reach, None])
        incoming = context_rows[row_start:key_reach]
        back_weights = right_transposed(incoming, value_rows[:key_reach])
        inner_sum = jnp.sum(probabilities * back_weights, axis=-1, keepdims=True)
        back_scores = (probabilities * (back_weights - inner_sum)).astype(jnp.bfloat16)
        query_parts.append(product(back_scores, key_rows[:key_reach]) * score_scale)
        key_total = key_total.at[:key_reach].add(
            left_transposed(back_scores, queries[row_start:key_reach]) * score_scale
        )
        value_total = value_total.at[:key_reach].add(
            left_transposed(probabilities.astype(jnp.bfloat16), incoming)
        )
    back_queries = jnp.concatenate(query_parts, axis=0).astype(jnp.bfloat16)
    return (back_queries, key_total.astype(jnp.bfloat16), value_total.astype(jnp.bfloat16))


def general_shards(
    inputs,
    block_ids,
    query_weight,
    query_bias,
    key_weight,
    value_weight,
    value_bias,
    output_weight,
    output_bias,
    attention_gain,
    attention_shift,
    expand_weight,
    expand_bias,
    reduce_weight,
    reduce_bias,
    final_gain,
    final_shift,
    cotangent,
):
    tokens = inputs[0]
    documents = block_ids[0]
    block_order = jnp.arange(documents.shape[0], dtype=jnp.int32)
    allowed = (documents[:, None] == documents[None, :]) & (
        block_order[None, :] <= block_order[:, None]
    )
    (
        query_full,
        query_shift,
        key_full,
        value_full,
        value_shift,
        output_full,
        output_shift,
        norm_gain,
        norm_shift,
        expand_full,
        expand_shift,
        reduce_full,
        reduce_shift,
        last_gain,
        last_shift,
    ) = (
        lax.all_gather(query_weight, "dp", axis=0, tiled=True),
        lax.all_gather(query_bias, "dp", axis=0, tiled=True),
        lax.all_gather(key_weight, "dp", axis=0, tiled=True),
        lax.all_gather(value_weight, "dp", axis=0, tiled=True),
        lax.all_gather(value_bias, "dp", axis=0, tiled=True),
        lax.all_gather(output_weight, "dp", axis=0, tiled=True),
        lax.all_gather(output_bias, "dp", axis=0, tiled=True),
        lax.all_gather(attention_gain, "dp", axis=0, tiled=True),
        lax.all_gather(attention_shift, "dp", axis=0, tiled=True),
        lax.all_gather(expand_weight, "dp", axis=0, tiled=True),
        lax.all_gather(expand_bias, "dp", axis=0, tiled=True),
        lax.all_gather(reduce_weight, "dp", axis=0, tiled=True),
        lax.all_gather(reduce_bias, "dp", axis=0, tiled=True),
        lax.all_gather(final_gain, "dp", axis=0, tiled=True),
        lax.all_gather(final_shift, "dp", axis=0, tiled=True),
    )
    queries_token = (product(tokens, query_full) + query_shift.astype(jnp.float32)).astype(
        jnp.bfloat16
    )
    keys_token = product(tokens, key_full).astype(jnp.bfloat16)
    values_token = (product(tokens, value_full) + value_shift.astype(jnp.float32)).astype(
        jnp.bfloat16
    )
    stacked = jnp.stack([queries_token, keys_token, values_token])
    spread_heads = lax.all_to_all(stacked, "seq", split_axis=2, concat_axis=1, tiled=True)
    length = spread_heads.shape[1]
    head_count = spread_heads.shape[2] // HD
    by_head = spread_heads.reshape(3, length, head_count, HD).transpose(0, 2, 1, 3)
    contexts, totals = lax.map(
        lambda head_item: head_forward(head_item, allowed), (by_head[0], by_head[1], by_head[2])
    )
    context_rows = contexts.transpose(1, 0, 2).reshape(length, head_count * HD)
    context_token = lax.all_to_all(
        as_sent(context_rows), "seq", split_axis=0, concat_axis=1, tiled=True
    ).astype(context_rows.dtype)
    attended = product(context_token, output_full) + output_shift.astype(jnp.float32)
    first_pre = tokens.astype(jnp.float32) + attended
    hidden, first_pull = jax.vjp(
        layer_norm, first_pre, norm_gain.astype(jnp.float32), norm_shift.astype(jnp.float32)
    )
    hidden_low = hidden.astype(jnp.bfloat16)
    expanded = product(hidden_low, expand_full) + expand_shift.astype(jnp.float32)
    activated, gelu_pull = jax.vjp(gelu_exact, expanded)
    activated_low = activated.astype(jnp.bfloat16)
    reduced = product(activated_low, reduce_full) + reduce_shift.astype(jnp.float32)
    final_pre = hidden_low.astype(jnp.float32) + reduced
    final_out, final_pull = jax.vjp(
        layer_norm, final_pre, last_gain.astype(jnp.float32), last_shift.astype(jnp.float32)
    )
    output = final_out.astype(jnp.bfloat16)[None]
    query_full, key_full, value_full, output_full, expand_full, reduce_full = (
        lax.all_gather(query_weight, "dp", axis=0, tiled=True),
        lax.all_gather(key_weight, "dp", axis=0, tiled=True),
        lax.all_gather(value_weight, "dp", axis=0, tiled=True),
        lax.all_gather(output_weight, "dp", axis=0, tiled=True),
        lax.all_gather(expand_weight, "dp", axis=0, tiled=True),
        lax.all_gather(reduce_weight, "dp", axis=0, tiled=True),
    )
    back_final, last_scale, last_offset = final_pull(cotangent[0].astype(jnp.float32))
    back_reduced = back_final.astype(jnp.bfloat16)
    reduce_matrix = left_transposed(activated_low, back_reduced)
    reduce_vector = column_sum(back_reduced)
    back_activated = right_transposed(back_reduced, reduce_full)
    back_expanded = gelu_pull(back_activated)[0].astype(jnp.bfloat16)
    expand_matrix = left_transposed(hidden_low, back_expanded)
    expand_vector = column_sum(back_expanded)
    back_hidden = back_final + right_transposed(back_expanded, expand_full)
    back_attended, first_scale, first_offset = first_pull(back_hidden)
    attended_low = back_attended.astype(jnp.bfloat16)
    output_matrix = left_transposed(context_token, attended_low)
    output_vector = column_sum(attended_low)
    back_context = right_transposed(attended_low, output_full).astype(jnp.bfloat16)
    context_spread = lax.all_to_all(back_context, "seq", split_axis=1, concat_axis=0, tiled=True)
    context_by_head = context_spread.reshape(length, head_count, HD).transpose(1, 0, 2)
    back_heads = lax.map(
        lambda head_item: head_backward(head_item, allowed),
        (by_head[0], by_head[1], by_head[2], context_by_head, totals),
    )
    back_stacked = jnp.stack(back_heads).transpose(0, 2, 1, 3).reshape(3, length, head_count * HD)
    back_token = lax.all_to_all(
        as_sent(back_stacked), "seq", split_axis=1, concat_axis=2, tiled=True
    ).astype(back_stacked.dtype)
    back_query = back_token[0]
    back_key = back_token[1]
    back_value = back_token[2]
    input_gradient = (
        back_attended
        + right_transposed(back_query, query_full)
        + right_transposed(back_key, key_full)
        + right_transposed(back_value, value_full)
    )
    query_matrix = left_transposed(tokens, back_query)
    query_vector = column_sum(back_query)
    key_matrix = left_transposed(tokens, back_key)
    value_matrix = left_transposed(tokens, back_value)
    value_vector = column_sum(back_value)
    (
        query_matrix,
        query_vector,
        key_matrix,
        value_matrix,
        value_vector,
        output_matrix,
        output_vector,
        first_scale,
        first_offset,
        expand_matrix,
        expand_vector,
        reduce_matrix,
        reduce_vector,
        last_scale,
        last_offset,
    ) = (
        lax.psum_scatter(query_matrix, "dp", scatter_dimension=0, tiled=True),
        lax.psum_scatter(query_vector, "dp", scatter_dimension=0, tiled=True),
        lax.psum_scatter(key_matrix, "dp", scatter_dimension=0, tiled=True),
        lax.psum_scatter(value_matrix, "dp", scatter_dimension=0, tiled=True),
        lax.psum_scatter(value_vector, "dp", scatter_dimension=0, tiled=True),
        lax.psum_scatter(output_matrix, "dp", scatter_dimension=0, tiled=True),
        lax.psum_scatter(output_vector, "dp", scatter_dimension=0, tiled=True),
        lax.psum_scatter(first_scale, "dp", scatter_dimension=0, tiled=True),
        lax.psum_scatter(first_offset, "dp", scatter_dimension=0, tiled=True),
        lax.psum_scatter(expand_matrix, "dp", scatter_dimension=0, tiled=True),
        lax.psum_scatter(expand_vector, "dp", scatter_dimension=0, tiled=True),
        lax.psum_scatter(reduce_matrix, "dp", scatter_dimension=0, tiled=True),
        lax.psum_scatter(reduce_vector, "dp", scatter_dimension=0, tiled=True),
        lax.psum_scatter(last_scale, "dp", scatter_dimension=0, tiled=True),
        lax.psum_scatter(last_offset, "dp", scatter_dimension=0, tiled=True),
    )
    owned = (
        lax.psum(query_matrix.astype(jnp.bfloat16), "seq").astype(jnp.float32),
        lax.psum(query_vector.astype(jnp.bfloat16), "seq").astype(jnp.float32),
        lax.psum(key_matrix.astype(jnp.bfloat16), "seq").astype(jnp.float32),
        lax.psum(value_matrix.astype(jnp.bfloat16), "seq").astype(jnp.float32),
        lax.psum(value_vector.astype(jnp.bfloat16), "seq").astype(jnp.float32),
        lax.psum(output_matrix.astype(jnp.bfloat16), "seq").astype(jnp.float32),
        lax.psum(output_vector.astype(jnp.bfloat16), "seq").astype(jnp.float32),
        lax.psum(first_scale.astype(jnp.bfloat16), "seq").astype(jnp.float32),
        lax.psum(first_offset.astype(jnp.bfloat16), "seq").astype(jnp.float32),
        lax.psum(expand_matrix.astype(jnp.bfloat16), "seq").astype(jnp.float32),
        lax.psum(expand_vector.astype(jnp.bfloat16), "seq").astype(jnp.float32),
        lax.psum(reduce_matrix.astype(jnp.bfloat16), "seq").astype(jnp.float32),
        lax.psum(reduce_vector.astype(jnp.bfloat16), "seq").astype(jnp.float32),
        lax.psum(last_scale.astype(jnp.bfloat16), "seq").astype(jnp.float32),
        lax.psum(last_offset.astype(jnp.bfloat16), "seq").astype(jnp.float32),
    )
    return (output, input_gradient[None]) + tuple(owned)


MESH = pl.DeviceIdType.MESH
KEY, VALUE, QUERY, OUT, EXPAND, REDUCE = range(6)
ROWS = (96, 96, 96, 96, 96, 384)
COLS = (768, 768, 768, 768, 3072, 768)
GATHER_UNITS = (
    [(w, 0, 768, False) for w in (KEY, VALUE, QUERY, OUT)]
    + [(EXPAND, 768 * j, 768, True) for j in range(4)]
    + [(REDUCE, 256 * j, 256, True) for j in range(3)]
)
SUM_UNITS = (
    [(REDUCE, 256 * j, 256) for j in range(3)]
    + [(EXPAND, 768 * j, 768) for j in range(4)]
    + [(w, 0, 768) for w in (OUT, QUERY, KEY, VALUE)]
)
TOKENS = 256
WIDTH = 768


class Place:
    def __init__(self):
        self.d = lax.axis_index("dp")
        self.z = lax.axis_index("seq")
        self.y = self.d // 4
        self.x = (self.d // 2) % 2
        self.c = self.d % 2
        self.parity = self.z % 2
        self.partner_z = self.z + 1 - 2 * self.parity

    def shard(self, flip_y, flip_x, flip_c):
        y = 1 - self.y if flip_y else self.y
        x = 1 - self.x if flip_x else self.x
        c = 1 - self.c if flip_c else self.c
        return 4 * y + 2 * x + c

    def quarter(self, flip_y, flip_x):
        y = 1 - self.y if flip_y else self.y
        x = 1 - self.x if flip_x else self.x
        return 2 * y + x

    def peer(self, kind):
        if kind == "x":
            return (self.shard(0, 1, 0), self.z)
        if kind == "y":
            return (self.shard(1, 0, 0), self.z)
        if kind == "s":
            return (self.shard(0, 0, 1), self.z)
        return (self.d, self.partner_z)


def remote(source, target, send_sem, recv_sem, peer):
    return pltpu.make_async_remote_copy(
        src_ref=source,
        dst_ref=target,
        send_sem=send_sem,
        recv_sem=recv_sem,
        device_id=peer,
        device_id_type=MESH,
    )


class Gather:
    def __init__(self, place, own, full, send_sems, recv_sems):
        self.place, self.own, self.full = place, own, full
        self.send_sems, self.recv_sems = send_sems, recv_sems

    def rows(self, unit, part):
        w, _, _, paired = GATHER_UNITS[unit]
        count = ROWS[w]
        parity = self.place.parity
        if part == "all":
            return pl.ds(0, count)
        if not paired:
            half = count // 2
            return {"a": pl.ds(0, half), "b": pl.ds(half, half), "ab": pl.ds(0, count)}[part]
        third = count // 3
        if part == "a":
            return pl.ds(pl.multiple_of(2 * third * parity, third), third)
        if part == "b":
            return pl.ds(third, third)
        if part == "w":
            return pl.ds(pl.multiple_of(2 * third * (1 - parity), third), third)
        return pl.ds(pl.multiple_of(third * parity, third), 2 * third)

    def slot(self, unit, shard, part):
        w, col, width, _ = GATHER_UNITS[unit]
        return self.full[w].at[shard, self.rows(unit, part), pl.ds(col, width)]

    def copy(self, unit, lane, kind, shard, part, source=None):
        target = self.slot(unit, shard, part)
        return remote(
            target if source is None else source,
            target,
            self.send_sems.at[unit, lane],
            self.recv_sems.at[unit, lane],
            self.place.peer(kind),
        )

    def own_source(self, unit, part):
        w, col, width, _ = GATHER_UNITS[unit]
        return self.own[w].at[self.rows(unit, part), pl.ds(col, width)]

    def sends(self, unit):
        p = self.place
        mine, over_x, over_y, over_d = p.d, p.shard(0, 1, 0), p.shard(1, 0, 0), p.shard(1, 1, 0)
        table = {
            0: ("x", mine, "ab", True),
            1: ("x", over_y, "a", False),
            2: ("y", mine, "ab", True),
            3: ("y", over_x, "b", False),
            4: ("s", mine, "all", True),
            5: ("s", over_x, "ab", False),
            6: ("s", over_y, "ab", False),
            7: ("s", over_d, "ab", False),
        }
        if GATHER_UNITS[unit][3]:
            table.update(
                {
                    8: ("z", over_x, "a", False),
                    9: ("z", over_y, "a", False),
                    10: ("z", over_d, "a", False),
                    11: ("s", over_x, "w", False),
                    12: ("s", over_y, "w", False),
                    13: ("s", over_d, "w", False),
                }
            )
        return table

    def arrivals(self, unit):
        p = self.place
        over_x, over_y, over_d = p.shard(0, 1, 0), p.shard(1, 0, 0), p.shard(1, 1, 0)
        sib, sib_x, sib_y, sib_d = p.shard(0, 0, 1), p.shard(0, 1, 1), p.shard(1, 0, 1), p.shard(1, 1, 1)
        return {
            0: ("x", over_x, "ab"),
            1: ("x", over_d, "a"),
            2: ("y", over_y, "ab"),
            3: ("y", over_d, "b"),
            4: ("s", sib, "all"),
            5: ("s", sib_x, "ab"),
            6: ("s", sib_y, "ab"),
            7: ("s", sib_d, "ab"),
            8: ("z", over_x, "w"),
            9: ("z", over_y, "w"),
            10: ("z", over_d, "w"),
            11: ("s", sib_x, "w"),
            12: ("s", sib_y, "w"),
            13: ("s", sib_d, "w"),
        }

    def start(self, unit, *lanes):
        table = self.sends(unit)
        for lane in lanes:
            if lane in table:
                kind, shard, part, from_own = table[lane]
                source = self.own_source(unit, part) if from_own else None
                self.copy(unit, lane, kind, shard, part, source).start()

    def wait(self, unit, *lanes):
        table = self.sends(unit)
        for lane in lanes:
            if lane in table:
                kind, shard, part = self.arrivals(unit)[lane]
                self.copy(unit, lane, kind, shard, part).wait_recv()

    def open(self, unit):
        if unit < len(GATHER_UNITS):
            self.start(unit, 0, 2, 4)

    def relay(self, unit):
        if 0 <= unit < len(GATHER_UNITS):
            self.wait(unit, 0)
            self.start(unit, 3, 8, 5)
            self.wait(unit, 2)
            self.start(unit, 1, 9, 6)

    def relay_far(self, unit):
        if 0 <= unit < len(GATHER_UNITS):
            self.wait(unit, 1)
            self.start(unit, 10)
            self.wait(unit, 3)
            self.start(unit, 7)
            self.wait(unit, 8)
            self.start(unit, 11)
            self.wait(unit, 9)
            self.start(unit, 12)

    def relay_last(self, unit):
        if 0 <= unit < len(GATHER_UNITS):
            self.wait(unit, 10)
            self.start(unit, 13)

    def arrived(self, unit):
        if 0 <= unit < len(GATHER_UNITS):
            self.wait(unit, 4, 5, 6, 7, 11, 12, 13)

    def drain(self):
        for unit in range(len(GATHER_UNITS)):
            for lane, (kind, shard, part, from_own) in self.sends(unit).items():
                source = self.own_source(unit, part) if from_own else None
                self.copy(unit, lane, kind, shard, part, source).wait_send()


PLANE = [(fy, fx, fc) for fy in (0, 1) for fx in (0, 1) for fc in (0, 1)][1:]


def greet(place):
    barrier = pltpu.get_barrier_semaphore()
    for flips in PLANE:
        pl.semaphore_signal(
            barrier, inc=1, device_id=(place.shard(*flips), place.z), device_id_type=MESH
        )

    @pl.when(place.z > 0)
    def _():
        pl.semaphore_signal(barrier, inc=1, device_id=(place.d, place.z - 1), device_id_type=MESH)

    @pl.when(place.z < 3)
    def _():
        pl.semaphore_signal(barrier, inc=1, device_id=(place.d, place.z + 1), device_id_type=MESH)

    pl.semaphore_wait(barrier, 8 + (place.z * (3 - place.z)) // 2)


def cut(unit, part):
    count = ROWS[SUM_UNITS[unit][0]]
    half = count // 2
    return {"a": pl.ds(0, half), "b": pl.ds(half, half), "all": pl.ds(0, count)}[part]


class Reduce:
    def __init__(self, place, buffers, out, send_sems, recv_sems, out_sems):
        self.place, self.out, self.out_sems = place, out, out_sems
        self.chip, self.far, self.near, self.outer, self.inner, self.total = buffers
        self.send_sems, self.recv_sems = send_sems, recv_sems
        self.rim_z = jnp.where(place.z < 2, 0, 3)
        self.core_z = jnp.where(place.z < 2, 1, 2)
        self.is_rim = (place.z == 0) | (place.z == 3)

    def view(self, family, unit, part, *lead):
        w, col, width = SUM_UNITS[unit]
        return family[w].at[(*lead, cut(unit, part), pl.ds(col, width))]

    def copy(self, unit, lane, source, target, peer):
        return remote(
            source, target, self.send_sems.at[unit, lane], self.recv_sems.at[unit, lane], peer
        )

    def sibling(self, unit, source):
        w, col, width = SUM_UNITS[unit]
        return self.copy(
            unit, 0, source, self.chip[w].at[:, :, pl.ds(col, width)], self.place.peer("s")
        )

    def lanes(self, unit):
        p = self.place
        to_x, to_y, to_d = p.quarter(0, 1), p.quarter(1, 0), p.quarter(1, 1)
        c, f, n = self.chip, self.far, self.near
        x, y = p.peer("x"), p.peer("y")
        return {
            1: (self.view(c, unit, "a", to_d), self.view(f, unit, "a"), x),
            2: (self.view(c, unit, "b", to_d), self.view(f, unit, "b"), y),
            3: (self.view(c, unit, "a", to_x), self.view(n, unit, "a", 0), x),
            4: (self.view(c, unit, "b", to_x), self.view(n, unit, "b", 0), x),
            5: (self.view(c, unit, "b", to_y), self.view(n, unit, "b", 1), y),
            6: (self.view(c, unit, "a", to_y), self.view(n, unit, "a", 1), y),
            7: (
                self.view(c, unit, "all", p.quarter(0, 0)),
                self.view(self.outer, unit, "all"),
                (p.d, self.core_z),
            ),
            8: (
                self.view(self.outer, unit, "all"),
                self.view(self.inner, unit, "all"),
                (p.d, 3 - self.core_z),
            ),
            9: (
                self.view(self.total, unit, "all"),
                self.view(self.total, unit, "all"),
                (p.d, self.rim_z),
            ),
        }

    def start(self, unit, *lanes):
        table = self.lanes(unit)
        for lane in lanes:
            self.copy(unit, lane, *table[lane]).start()

    def wait(self, unit, *lanes):
        table = self.lanes(unit)
        for lane in lanes:
            self.copy(unit, lane, *table[lane]).wait_recv()

    def chip_sum(self, unit, add_own):
        if not 0 <= unit < len(SUM_UNITS):
            return
        w, col, width = SUM_UNITS[unit]
        self.sibling(unit, self.chip[w].at[:, :, pl.ds(col, width)]).wait_recv()
        add_own()
        self.start(unit, 1, 2, 3, 5)

    def relay(self, unit):
        if not 0 <= unit < len(SUM_UNITS):
            return
        p = self.place
        for lane, part, quarter, after in (
            (1, "a", p.quarter(1, 0), 6),
            (2, "b", p.quarter(0, 1), 4),
        ):
            self.wait(unit, lane)
            target = self.view(self.chip, unit, part, quarter)
            target[...] = (
                target[...].astype(jnp.float32)
                + self.view(self.far, unit, part)[...].astype(jnp.float32)
            ).astype(jnp.bfloat16)
            self.start(unit, after)

    def plane_sum(self, unit):
        if not 0 <= unit < len(SUM_UNITS):
            return
        mine = self.place.quarter(0, 0)
        self.wait(unit, 3, 4, 5, 6)
        total = self.view(self.chip, unit, "all", mine)[...].astype(jnp.float32)
        for side in (0, 1):
            total = total + self.view(self.near, unit, "all", side)[...].astype(jnp.float32)
        self.view(self.chip, unit, "all", mine)[...] = total.astype(jnp.bfloat16)

        @pl.when(self.is_rim)
        def _():
            self.start(unit, 7)

    def half_sum(self, unit):
        if not 0 <= unit < len(SUM_UNITS):
            return

        @pl.when(jnp.logical_not(self.is_rim))
        def _():
            self.wait(unit, 7)
            self.view(self.outer, unit, "all")[...] = (
                self.view(self.chip, unit, "all", self.place.quarter(0, 0))[...].astype(jnp.float32)
                + self.view(self.outer, unit, "all")[...].astype(jnp.float32)
            ).astype(jnp.bfloat16)
            self.start(unit, 8)

    def full_sum(self, unit):
        if not 0 <= unit < len(SUM_UNITS):
            return

        @pl.when(jnp.logical_not(self.is_rim))
        def _():
            self.wait(unit, 8)
            self.view(self.total, unit, "all")[...] = (
                self.view(self.outer, unit, "all")[...].astype(jnp.float32)
                + self.view(self.inner, unit, "all")[...].astype(jnp.float32)
            ).astype(jnp.bfloat16)
            self.start(unit, 9)

    def result(self, unit):
        return pltpu.make_async_copy(
            self.view(self.total, unit, "all"), self.view(self.out, unit, "all"), self.out_sems.at[unit]
        )

    def collect(self, unit):
        if not 0 <= unit < len(SUM_UNITS):
            return

        @pl.when(self.is_rim)
        def _():
            self.wait(unit, 9)

        self.result(unit).start()

    def finish(self):
        units = range(len(SUM_UNITS))

        for unit in units:
            self.result(unit).wait()
            table = self.lanes(unit)
            for lane in range(1, 7):
                self.copy(unit, lane, *table[lane]).wait_send()

        @pl.when(self.is_rim)
        def _():
            for unit in units:
                self.copy(unit, 7, *self.lanes(unit)[7]).wait_send()

        @pl.when(jnp.logical_not(self.is_rim))
        def _():
            for unit in units:
                for lane in (8, 9):
                    self.copy(unit, lane, *self.lanes(unit)[lane]).wait_send()


class VectorSum:
    def __init__(self, place, reduce, current, parts, send_sems, recv_sems):
        self.current, self.parts = current, parts
        self.send_sems, self.recv_sems = send_sems, recv_sems
        self.is_rim = reduce.is_rim
        self.is_core = jnp.logical_not(reduce.is_rim)
        self.peers = [place.peer(kind) for kind in "sxy"] + [
            (place.d, reduce.core_z),
            (place.d, 3 - place.z),
            (place.d, reduce.rim_z),
        ]

    def copy(self, step):
        return remote(
            self.current.at[step],
            self.parts.at[step],
            self.send_sems.at[step],
            self.recv_sems.at[step],
            self.peers[step],
        )

    def take(self, step):
        self.copy(step).wait_recv()
        self.current[step + 1] = self.current[step] + self.parts[step]

    def phase(self, number):
        if number == 0:
            self.copy(0).start()
        elif number < 3:
            self.take(number - 1)
            self.copy(number).start()
        elif number == 3:
            self.take(2)

            @pl.when(self.is_rim)
            def _():
                self.copy(3).start()

        elif number in (4, 5):

            @pl.when(self.is_core)
            def _():
                self.take(number - 1)
                self.copy(number).start()
                if number == 5:
                    self.current[6] = self.current[5]

        else:

            @pl.when(self.is_rim)
            def _():
                self.copy(5).wait_recv()
                self.current[6] = self.parts[5]
                self.copy(3).wait_send()

            for step in range(3):
                self.copy(step).wait_send()

            @pl.when(self.is_core)
            def _():
                self.copy(4).wait_send()
                self.copy(5).wait_send()


def chunk(index, size):
    return pl.ds(pl.multiple_of(index * size, size), size)


def loop(count, body):
    def step(index, carry):
        body(index)
        return carry

    lax.fori_loop(0, count, step, 0)


def fold_rows(values):
    return values[0:8] + values[8:16] + values[16:24] + values[24:32]


def layer_kernel(*refs):
    own = refs[:6]
    vectors, tokens, cotangent, block_ids = refs[6:10]
    output_hbm, gradient_hbm = refs[10:12]
    totals_hbm, vector_total = refs[12:18], refs[18]
    refs = refs[19:]
    full, refs = refs[:6], refs[6:]
    families = [refs[6 * i : 6 * (i + 1)] for i in range(6)]
    refs = refs[36:]
    (
        ring_reduce,
        ring_other,
        all_vectors,
        vecs,
        expand_shift,
        blocks,
        tangent,
        reach_t,
        queries,
        keys,
        values,
        keys_t,
        values_t,
        weights_t,
        context_t,
        context,
        first_norm,
        first_rate,
        hidden,
        hidden_t,
        active,
        active_t,
        slope,
        back_reduced,
        attended_low,
        back_context,
        back_query_t,
        back_query,
        back_key,
        spread_send,
        spread_recv,
        sums,
        expand_sum,
        current,
        parts,
        output,
        gradient,
    ) = refs[:37]
    (
        local_sems,
        gather_send,
        gather_recv,
        vec_send,
        vec_recv,
        tok_send,
        tok_recv,
        sum_send,
        sum_recv,
        small_send,
        small_recv,
        spread_ssem,
        spread_rsem,
        out_sems,
    ) = refs[37:]
    back_expanded = active
    back_value = values_t
    f32, low = jnp.float32, jnp.bfloat16
    place = Place()
    gather = Gather(place, own, full, gather_send, gather_recv)
    reduce = Reduce(place, families, totals_hbm, sum_send, sum_recv, out_sems)
    output_copy = pltpu.make_async_copy(output, output_hbm, local_sems.at[9])
    gradient_copy = pltpu.make_async_copy(gradient, gradient_hbm, local_sems.at[10])
    small = VectorSum(place, reduce, current, parts, small_send, small_recv)
    local = [pltpu.make_async_copy(own[w], full[w].at[place.d], local_sems.at[w]) for w in range(6)]
    local.append(pltpu.make_async_copy(vectors, all_vectors.at[place.d], local_sems.at[6]))
    local.append(pltpu.make_async_copy(tokens.at[0], blocks.at[2], local_sems.at[7]))
    local.append(pltpu.make_async_copy(cotangent.at[0], tangent, local_sems.at[8]))
    for copy in local:
        copy.start()
    greet(place)

    def tick(unit):
        gather.relay(unit)
        gather.open(unit + 2)
        gather.relay_far(unit - 1)
        gather.relay_last(unit - 2)

    def vector_copy(i, shard, peer):
        return remote(vectors, all_vectors.at[shard], vec_send.at[i], vec_recv.at[i], peer)

    def token_copy(slot, source, peer_z):
        return remote(
            source, blocks.at[slot], tok_send.at[slot], tok_recv.at[slot], (place.d, peer_z)
        )

    for i, flips in enumerate(PLANE):
        vector_copy(i, place.d, (place.shard(*flips), place.z)).start()

    @pl.when(place.z < 3)
    def _():
        token_copy(1, tokens.at[0], place.z + 1).start()

    for unit in range(2):
        gather.open(unit)

    @pl.when(place.z == 0)
    def _():
        blocks[0] = jnp.zeros((TOKENS, WIDTH), low)
        blocks[1] = jnp.zeros((TOKENS, WIDTH), low)

    @pl.when(place.z == 1)
    def _():
        blocks[0] = jnp.zeros((TOKENS, WIDTH), low)

    for copy in local:
        copy.wait()

    def turn(slot):
        reach_t[:, slot * TOKENS : (slot + 1) * TOKENS] = blocks[slot].T

    turn(2)
    sums[...] = jnp.zeros_like(sums)
    tick(0)

    @pl.when(place.z > 0)
    def _():
        token_copy(1, tokens.at[0], place.z - 1).wait_recv()

        @pl.when(place.z < 3)
        def _():
            token_copy(0, blocks.at[1], place.z + 1).start()

    turn(1)
    for i, flips in enumerate(PLANE):
        vector_copy(i, place.shard(*flips), (place.shard(*flips), place.z)).wait_recv()

    def place_vectors(s, total):
        row = lax.broadcasted_iota(jnp.int32, (128, WIDTH), 0)
        lane = lax.broadcasted_iota(jnp.int32, (128, WIDTH), 1)
        pick = jnp.where((lane == row + 96 * s) & (row < 96), 1.0, 0.0).astype(low)
        return total + product(all_vectors[s], pick)

    vecs[...] = lax.fori_loop(0, 8, place_vectors, jnp.zeros((16, WIDTH), f32))
    for s in range(8):
        rows = all_vectors[s].astype(f32)
        for r in range(3):
            expand_shift[:, 384 * s + 128 * r : 384 * s + 128 * (r + 1)] = rows[8 + r : 9 + r, :]
    tick(1)

    def weight_columns(w, cols):
        return full[w][:, :, cols].reshape(8 * ROWS[w], 256)

    def project_keys(first, count):
        def body(i):
            cols = chunk(i, 256)
            source = blocks[first : first + count].reshape(count * TOKENS, WIDTH)
            part = product(source, weight_columns(KEY, cols)).astype(low)
            toks = slice(first * TOKENS, (first + count) * TOKENS)
            keys[toks, cols] = part
            keys_t[cols, toks] = part.T

        loop(3, body)

    def project_values(first, count):
        def body(i):
            cols = chunk(i, 256)
            source = blocks[first : first + count].reshape(count * TOKENS, WIDTH)
            part = (product(source, weight_columns(VALUE, cols)) + vecs[1:2, cols]).astype(low)
            toks = slice(first * TOKENS, (first + count) * TOKENS)
            values[toks, cols] = part
            values_t[cols, toks] = part.T

        loop(3, body)

    gather.arrived(0)
    project_keys(1, 2)
    tick(2)
    gather.arrived(1)
    project_values(1, 2)

    @pl.when(place.z > 1)
    def _():
        token_copy(0, blocks.at[1], place.z - 1).wait_recv()

    tick(3)
    turn(0)
    project_keys(0, 1)
    project_values(0, 1)
    gather.arrived(2)

    def project_queries(i):
        cols = chunk(i, 256)
        part = (product(blocks[2], weight_columns(QUERY, cols)) + vecs[0:1, cols]).astype(low)
        queries[:, cols] = (part.astype(f32) * HD ** (-0.5)).astype(low)

    loop(3, project_queries)

    mine = block_ids[0, place.z]
    biases = []
    for slot in range(2):
        source = place.z - 2 + slot
        seen = (source >= 0) & (block_ids[0, jnp.maximum(source, 0)] == mine)
        biases.append(jnp.where(seen, 0.0, MASKED).astype(f32))

    def half_lanes(values, half):
        lane = lax.broadcasted_iota(jnp.int32, values.shape, 1)
        keep = (lane >= 64) if half else (lane < 64)
        return jnp.where(keep, values, jnp.zeros_like(values))

    def attend(first, count):
        def body(i):
            pair = first + i
            cols = chunk(pair, 128)
            pair_queries = queries[:, cols]
            for half in range(2):
                masked = half_lanes(pair_queries, half)
                scores = [
                    right_transposed(keys[slot * TOKENS : (slot + 1) * TOKENS, cols], masked)
                    for slot in range(3)
                ]
                scores = [scores[0] + biases[0], scores[1] + biases[1], scores[2]]
                peak = jnp.maximum(
                    jnp.maximum(
                        jnp.max(scores[0], axis=0, keepdims=True),
                        jnp.max(scores[1], axis=0, keepdims=True),
                    ),
                    jnp.max(scores[2], axis=0, keepdims=True),
                )
                powers = [jnp.exp(s - peak) for s in scores]
                total = sum(jnp.sum(p, axis=0, keepdims=True) for p in powers)
                share = 1.0 / total
                for slot in range(3):
                    weights_t[2 * pair + half, slot * TOKENS : (slot + 1) * TOKENS, :] = (
                        powers[slot] * share
                    ).astype(low)
                rows = pl.ds(pl.multiple_of(pair * 128 + half * 64, 64), 64)
                context_t[rows, :] = product(values_t[rows, :], weights_t[2 * pair + half]).astype(
                    low
                )

        loop(count, body)

    attend(0, 2)
    tick(4)
    attend(2, 2)
    tick(5)
    attend(4, 2)
    gather.arrived(3)

    def project_output(i):
        cols = chunk(i, 256)
        if True:
            part = product(context[...], weight_columns(OUT, cols)) + vecs[2:3, cols]
        gradient[:, cols] = part + blocks[2, :, cols].astype(f32)

    context[...] = context_t[...].T
    loop(3, project_output)

    def mean(values):
        return jnp.sum(values, axis=-1, keepdims=True) * (1.0 / WIDTH)

    def first_normalise(i):
        rows = chunk(i, 32)
        values = gradient[rows, :]
        centred = values - mean(values)
        rate = lax.rsqrt(mean(centred * centred) + EPSILON)
        norm = centred * rate
        first_norm[rows, :] = norm
        first_rate[rows, :] = jnp.broadcast_to(rate, (32, 128))
        hidden[rows, :] = (norm * vecs[3:4, :] + vecs[4:5, :]).astype(low)

    loop(8, first_normalise)
    hidden_t[...] = hidden[...].T
    tick(6)

    def expand(unit):
        def body(i):
            cols = chunk(3 * unit + i, 256)
            inner = product(hidden[...], weight_columns(EXPAND, cols)) + expand_shift[:, cols]
            share = 0.5 * (1.0 + lax.erf(inner * 0.7071067811865476))
            bell = jnp.exp(inner * inner * -0.5) * 0.3989422804014327
            act = (inner * share).astype(low)
            active[:, cols] = act
            active_t[cols, :] = act.T
            slope[:, cols] = (share + inner * bell).astype(low)

        loop(3, body)

    for j in range(4):
        gather.arrived(4 + j)
        expand(j)
        tick(7 + j)

    for j in range(3):
        if j:
            tick(10 + j)
        gather.arrived(8 + j)
        cols = slice(256 * j, 256 * (j + 1))
        part = product(active[...], full[REDUCE][:, :, cols].reshape(3072, 256))
        gradient[:, cols] = part + vecs[5:6, cols] + hidden[:, cols].astype(f32)

    def last_normalise(i):
        rows = chunk(i, 32)
        values = gradient[rows, :]
        centred = values - mean(values)
        rate = lax.rsqrt(mean(centred * centred) + EPSILON)
        norm = centred * rate
        output[rows, :] = (norm * vecs[6:7, :] + vecs[7:8, :]).astype(low)
        arriving = tangent[rows, :].astype(f32)
        sums[0] += fold_rows(arriving * norm)
        sums[1] += fold_rows(arriving)
        scaled = arriving * vecs[6:7, :]
        back = (scaled - mean(scaled) - norm * mean(scaled * norm)) * rate
        gradient[rows, :] = back
        rounded = back.astype(low)
        back_reduced[rows, :] = rounded
        sums[2] += fold_rows(rounded.astype(f32))

    loop(8, last_normalise)
    output_copy.start()

    def shard_rows(shard, count):
        return pl.ds(pl.multiple_of(shard * count, 32), count)

    def group(source, parity, toks=None):
        picks = []
        for quarter in range(4):
            rows = shard_rows(2 * quarter + parity, 96)
            picks.append(source[rows, :] if toks is None else source[rows, toks])
        return jnp.concatenate(picks, axis=0)

    def terms(unit, parity, put):
        w, col, width = SUM_UNITS[unit]
        first = col // 256
        if w == REDUCE:

            def body(quarter):
                rows = shard_rows(2 * quarter + parity, 384)
                put(quarter, 0, product(active_t[rows, :], back_reduced[:, col : col + 256]))

            loop(4, body)
            return

        if w == EXPAND:
            lhs, rhs = (lambda: group(hidden_t, parity)), back_expanded
        elif w == OUT:
            lhs, rhs = (lambda: group(context_t, parity)), attended_low
        elif w == QUERY:
            lhs, rhs = (lambda: group(reach_t, parity, slice(512, 768))), back_query
        else:
            lhs, rhs = (lambda: group(reach_t, parity)), back_key if w == KEY else back_value

        def body(i):
            term = product(lhs(), rhs[:, chunk(first + i, 256)])
            for quarter in range(4):
                put(quarter, i, term[96 * quarter : 96 * (quarter + 1)])

        loop(width // 256, body)

    def slot_of(unit):
        if unit < 3:
            return ring_reduce.at[unit % 2]
        return ring_other.at[(unit - 3) % 3, :, :, pl.ds(0, SUM_UNITS[unit][2])]

    def ring_before(unit):
        return unit - 2 if unit == 2 else (unit - 3 if unit >= 6 else None)

    def send_half(unit):
        if unit >= len(SUM_UNITS):
            return
        earlier = ring_before(unit)
        if earlier is not None:
            reduce.sibling(earlier, slot_of(earlier)).wait_send()
        ring = ring_reduce.at[unit % 2] if unit < 3 else ring_other.at[(unit - 3) % 3]

        def put(quarter, i, term):
            ring[quarter, :, chunk(i, 256)] = term.astype(low)

        terms(unit, 1 - place.c, put)
        reduce.sibling(unit, slot_of(unit)).start()

    def own_half(unit):
        if unit >= len(SUM_UNITS):
            return
        w, col, width = SUM_UNITS[unit]

        def add_own():
            def put(quarter, i, term):
                where = (quarter, slice(None), chunk(col // 256 + i, 256))
                reduce.chip[w][where] = (term + reduce.chip[w][where].astype(f32)).astype(low)

            terms(unit, place.c, put)

        reduce.chip_sum(unit, add_own)

    def step(unit):
        own_half(unit)
        reduce.relay(unit - 1)
        reduce.plane_sum(unit - 2)
        reduce.half_sum(unit - 3)
        reduce.full_sum(unit - 4)
        reduce.collect(unit - 7)

    def back_expand(j):
        def body(i):
            shard = 2 * j + i
            cols = pl.ds(pl.multiple_of(shard * 384, 128), 384)
            back = right_transposed(back_reduced[...], full[REDUCE][shard])
            rounded = (back * slope[:, cols].astype(f32)).astype(low)
            back_expanded[:, cols] = rounded
            expand_sum[:, cols] = jnp.sum(rounded.astype(f32), axis=0, keepdims=True)

        loop(2, body)

        def gather_hidden(i):
            cols = slice(768 * j, 768 * (j + 1))
            rows = full[EXPAND][pl.ds(4 * i, 4), :, cols].reshape(384, 768)
            out = pl.ds(pl.multiple_of(i * 384, 128), 384)
            gradient[:, out] += right_transposed(back_expanded[:, cols], rows)

        loop(2, gather_hidden)

    send_half(0)
    send_half(1)
    step(0)
    back_expand(0)
    send_half(2)
    step(1)
    back_expand(1)
    send_half(3)
    step(2)
    back_expand(2)
    send_half(4)
    step(3)
    back_expand(3)
    send_half(5)
    step(4)

    def first_back(i):
        rows = chunk(i, 32)
        back = gradient[rows, :]
        norm = first_norm[rows, :]
        sums[3] += fold_rows(back * norm)
        sums[4] += fold_rows(back)
        scaled = back * vecs[3:4, :]
        rate = first_rate[rows, 0:1]
        back = (scaled - mean(scaled) - norm * mean(scaled * norm)) * rate
        gradient[rows, :] = back
        rounded = back.astype(low)
        attended_low[rows, :] = rounded
        sums[5] += fold_rows(rounded.astype(f32))

    loop(8, first_back)

    def weight_rows(w, i):
        return full[w][pl.ds(4 * i, 4), :, :].reshape(384, WIDTH)

    def back_output(i):
        out = pl.ds(pl.multiple_of(i * 384, 128), 384)
        back_context[:, out] = right_transposed(attended_low[...], weight_rows(OUT, i)).astype(low)

    loop(2, back_output)
    send_half(6)
    step(5)

    def attend_back(first, count):
        def body(i):
            pair = first + i
            cols = chunk(pair, 128)
            pair_back = back_context[:, cols]
            pair_queries = queries[:, cols]
            key_term, value_term = 0.0, 0.0
            for half in range(2):
                masked = half_lanes(pair_back, half)
                weights = weights_t[2 * pair + half].astype(f32)
                back = right_transposed(values[:, cols], masked)
                inner = jnp.sum(weights * back, axis=0, keepdims=True)
                back_scores = (weights * (back - inner)).astype(low)
                key_term += product(back_scores, half_lanes(pair_queries, half))
                value_term += product(weights_t[2 * pair + half], masked)
                rows = pl.ds(pl.multiple_of(pair * 128 + half * 64, 64), 64)
                back_query_t[rows, :] = (
                    product(keys_t[rows, :], back_scores) * HD ** (-0.5)
                ).astype(low)
            back_key[:, cols] = key_term.astype(low)
            back_value[:, cols] = value_term.astype(low)

        loop(count, body)

    attend_back(0, 3)
    send_half(7)
    step(6)
    attend_back(3, 3)
    back_query[...] = back_query_t[...].T
    send_half(8)
    step(7)

    def spread_copy(slot):
        return remote(
            spread_send.at[slot],
            spread_recv.at[slot],
            spread_ssem.at[slot],
            spread_rsem.at[slot],
            (place.d, place.z - 1),
        )

    def spread_into(block):
        toks = slice(block * TOKENS, (block + 1) * TOKENS)

        def body(i):
            out = pl.ds(pl.multiple_of(i * 384, 128), 384)
            part = right_transposed(back_key[toks, :], weight_rows(KEY, i)) + right_transposed(
                back_value[toks, :], weight_rows(VALUE, i)
            )
            if block == 2:
                part = part + right_transposed(back_query[...], weight_rows(QUERY, i))
                gradient[:, out] += part
            else:
                spread_send[block, :, out] = part.astype(low)

        loop(2, body)

    spread_into(0)

    @pl.when(place.z > 1)
    def _():
        spread_copy(0).start()

    spread_into(1)

    @pl.when(place.z == 3)
    def _():
        spread_copy(1).start()

    def column_total(values):
        return jnp.sum(values, axis=0, keepdims=True)

    rows = [
        column_total(back_query[...].astype(f32)),
        column_total(back_value[...].astype(f32)),
        column_total(sums[5]),
        column_total(sums[3]),
        column_total(sums[4]),
        column_total(sums[2]),
        column_total(sums[0]),
        column_total(sums[1]),
    ] + [expand_sum[:, WIDTH * i : WIDTH * (i + 1)] for i in range(4)]
    for i, row in enumerate(rows):
        current[0, i : i + 1, :] = row
    current[0, 12:16, :] = jnp.zeros((4, WIDTH), f32)
    small.phase(0)
    send_half(9)
    step(8)
    small.phase(1)

    @pl.when((place.z > 0) & (place.z < 3))
    def _():
        pltpu_copy = remote(
            spread_send.at[0],
            spread_recv.at[0],
            spread_ssem.at[0],
            spread_rsem.at[0],
            (place.d, place.z + 1),
        )
        pltpu_copy.wait_recv()
        spread_send[1] = (spread_send[1].astype(f32) + spread_recv[0].astype(f32)).astype(low)
        spread_copy(1).start()

    spread_into(2)
    send_half(10)
    step(9)
    small.phase(2)
    step(10)
    small.phase(3)
    send_half(12)
    step(11)
    small.phase(4)
    step(12)
    small.phase(5)
    step(13)

    @pl.when(place.z < 3)
    def _():
        remote(
            spread_send.at[1],
            spread_recv.at[1],
            spread_ssem.at[1],
            spread_rsem.at[1],
            (place.d, place.z + 1),
        ).wait_recv()

        def body(i):
            rows = chunk(i, 32)
            gradient[rows, :] += spread_recv[1, rows, :].astype(f32)

        loop(8, body)

    gradient_copy.start()
    step(14)
    step(15)
    step(16)
    small.phase(6)
    step(17)
    step(18)
    step(19)
    vector_total[...] = current[6]

    gather.drain()
    for i, flips in enumerate(PLANE):
        vector_copy(i, place.d, (place.shard(*flips), place.z)).wait_send()

    @pl.when(place.z < 3)
    def _():
        token_copy(1, tokens.at[0], place.z + 1).wait_send()

    @pl.when((place.z > 0) & (place.z < 3))
    def _():
        token_copy(0, blocks.at[1], place.z + 1).wait_send()

    @pl.when(place.z > 1)
    def _():
        spread_copy(0).wait_send()

    @pl.when(place.z > 0)
    def _():
        spread_copy(1).wait_send()

    waited = [ring_before(unit) for unit in range(len(SUM_UNITS))]
    for unit in range(len(SUM_UNITS)):
        if unit not in waited:
            reduce.sibling(unit, slot_of(unit)).wait_send()
    reduce.finish()
    output_copy.wait()
    gradient_copy.wait()


def layer_call(weights, vectors, tokens, cotangent, block_ids):
    hbm = pl.BlockSpec(memory_space=pl.ANY)
    vmem = pl.BlockSpec(memory_space=pltpu.VMEM)
    dma = pltpu.SemaphoreType.DMA
    low, f32 = jnp.bfloat16, jnp.float32
    gathers, units = len(GATHER_UNITS), len(SUM_UNITS)

    def family(*lead):
        return [pltpu.VMEM((*lead, ROWS[w], COLS[w]), low) for w in range(6)]

    def wide(rows, cols, kind=low):
        return pltpu.VMEM((rows, cols), kind)

    scratch = (
        family(8)
        + family(4)
        + family()
        + family(2)
        + family()
        + family()
        + family()
        + [
            pltpu.VMEM((2, 4, 384, 256), low),
            pltpu.VMEM((3, 4, 96, WIDTH), low),
            pltpu.VMEM((8, 16, 128), low),
            wide(16, WIDTH, f32),
            wide(1, 3072, f32),
            pltpu.VMEM((3, TOKENS, WIDTH), low),
            wide(TOKENS, WIDTH),
            wide(WIDTH, 3 * TOKENS),
            wide(TOKENS, WIDTH),
            wide(3 * TOKENS, WIDTH),
            wide(3 * TOKENS, WIDTH),
            wide(WIDTH, 3 * TOKENS),
            wide(WIDTH, 3 * TOKENS),
            pltpu.VMEM((12, 3 * TOKENS, TOKENS), low),
            wide(WIDTH, TOKENS),
            wide(TOKENS, WIDTH),
            wide(TOKENS, WIDTH, f32),
            wide(TOKENS, 128, f32),
            wide(TOKENS, WIDTH),
            wide(WIDTH, TOKENS),
            wide(TOKENS, 3072),
            wide(3072, TOKENS),
            wide(TOKENS, 3072),
            wide(TOKENS, WIDTH),
            wide(TOKENS, WIDTH),
            wide(TOKENS, WIDTH),
            wide(WIDTH, TOKENS),
            wide(TOKENS, WIDTH),
            wide(3 * TOKENS, WIDTH),
            pltpu.VMEM((2, TOKENS, WIDTH), low),
            pltpu.VMEM((2, TOKENS, WIDTH), low),
            pltpu.VMEM((6, 8, WIDTH), f32),
            wide(1, 3072, f32),
            pltpu.VMEM((7, 16, WIDTH), f32),
            pltpu.VMEM((6, 16, WIDTH), f32),
            wide(TOKENS, WIDTH),
            wide(TOKENS, WIDTH, f32),
            dma((11,)),
            dma((gathers, 14)),
            dma((gathers, 14)),
            dma((7,)),
            dma((7,)),
            dma((2,)),
            dma((2,)),
            dma((units, 10)),
            dma((units, 10)),
            dma((6,)),
            dma((6,)),
            dma((2,)),
            dma((2,)),
            dma((units,)),
        ]
    )
    return pl.pallas_call(
        layer_kernel,
        out_shape=[
            jax.ShapeDtypeStruct((TOKENS, WIDTH), low),
            jax.ShapeDtypeStruct((TOKENS, WIDTH), f32),
        ]
        + [jax.ShapeDtypeStruct((ROWS[w], COLS[w]), low) for w in range(6)]
        + [jax.ShapeDtypeStruct((16, WIDTH), f32)],
        in_specs=[hbm] * 9 + [pl.BlockSpec(memory_space=pltpu.SMEM)],
        out_specs=[hbm] * 8 + [vmem],
        scratch_shapes=scratch,
        compiler_params=pltpu.CompilerParams(
            collective_id=0, has_side_effects=True, vmem_limit_bytes=67043328
        ),
        name="layer",
    )(*weights, vectors, tokens, cotangent, block_ids)


def finish_kernel(*refs):
    passed, sums, vectors = refs[:2], refs[2:8], refs[8]
    passed_out, sums_out, small_out, expand_out = refs[9:11], refs[11:17], refs[17:25], refs[25]
    passed_buf, sums_buf, wide_buf = refs[26:28], refs[28:34], refs[34:40]
    in_sems, out_sems = refs[40:]
    order = [REDUCE, EXPAND, OUT, QUERY, KEY, VALUE]
    loads = [pltpu.make_async_copy(sums[w], sums_buf[w], in_sems.at[w]) for w in range(6)]
    stores = [pltpu.make_async_copy(wide_buf[w], sums_out[w], out_sems.at[w]) for w in range(6)]
    for i in range(2):
        loads.append(pltpu.make_async_copy(passed[i], passed_buf[i], in_sems.at[6 + i]))
        stores.append(pltpu.make_async_copy(passed_buf[i], passed_out[i], out_sems.at[6 + i]))
    for w in order + [6, 7]:
        loads[w].start()
    d = lax.axis_index("dp")
    turned = pltpu.roll(vectors[0:8, :], lax.rem(WIDTH - 96 * d, WIDTH), 1)
    for i in range(8):
        small_out[i][...] = turned[i, 0:96]
    expand_row = vectors[pl.ds(8 + d // 2, 1), pl.ds(pl.multiple_of(384 * (d % 2), 128), 384)]
    expand_out[...] = expand_row[0]
    for w in order:
        loads[w].wait()
        wide_buf[w][...] = sums_buf[w][...].astype(jnp.float32)
        stores[w].start()
    for i in (6, 7):
        loads[i].wait()
        stores[i].start()
    for store in stores:
        store.wait()


def finish_call(output, gradient, totals, vectors):
    hbm = pl.BlockSpec(memory_space=pl.ANY)
    vmem = pl.BlockSpec(memory_space=pltpu.VMEM)
    low, f32 = jnp.bfloat16, jnp.float32
    passed = [jax.ShapeDtypeStruct((TOKENS, WIDTH), kind) for kind in (low, f32)]
    sums = [jax.ShapeDtypeStruct((ROWS[w], COLS[w]), f32) for w in range(6)]
    return pl.pallas_call(
        finish_kernel,
        out_shape=passed
        + sums
        + [jax.ShapeDtypeStruct((96,), f32)] * 8
        + [jax.ShapeDtypeStruct((384,), f32)],
        in_specs=[hbm] * 8 + [vmem],
        out_specs=[hbm] * 8 + [vmem] * 9,
        scratch_shapes=[pltpu.VMEM(s.shape, s.dtype) for s in passed]
        + [pltpu.VMEM(s.shape, low) for s in sums]
        + [pltpu.VMEM(s.shape, f32) for s in sums]
        + [pltpu.SemaphoreType.DMA((8,))] * 2,
        name="finish",
    )(output, gradient, *totals, vectors)


def fitted_shards(
    inputs,
    block_ids,
    query_weight,
    query_bias,
    key_weight,
    value_weight,
    value_bias,
    output_weight,
    output_bias,
    attention_gain,
    attention_shift,
    expand_weight,
    expand_bias,
    reduce_weight,
    reduce_bias,
    final_gain,
    final_shift,
    cotangent,
):
    low = jnp.bfloat16
    small = [
        query_bias,
        value_bias,
        output_bias,
        attention_gain,
        attention_shift,
        reduce_bias,
        final_gain,
        final_shift,
    ]
    packed = jnp.concatenate(
        [
            jnp.pad(jnp.stack(small), ((0, 0), (0, 32))),
            expand_bias.reshape(3, 128),
            jnp.zeros((5, 128), low),
        ]
    )
    output, gradient, *totals, vector_total = layer_call(
        (key_weight, value_weight, query_weight, output_weight, expand_weight, reduce_weight),
        packed,
        inputs,
        cotangent,
        block_ids,
    )
    done = finish_call(output, gradient, totals, vector_total)
    output, gradient = done[:2]
    key_sum, value_sum, query_sum, output_sum, expand_sum, reduce_sum = done[2:8]
    small_sums, expand_part = done[8:16], done[16]
    return (
        output[None],
        gradient[None],
        query_sum,
        small_sums[0],
        key_sum,
        value_sum,
        small_sums[1],
        output_sum,
        small_sums[2],
        small_sums[3],
        small_sums[4],
        expand_sum,
        expand_part,
        reduce_sum,
        small_sums[5],
        small_sums[6],
        small_sums[7],
    )


def solution(mesh):
    placed = (
        P("dp", "seq", None),
        P("dp", None),
        P("dp", None),
        P("dp"),
        P("dp", None),
        P("dp", None),
        P("dp"),
        P("dp", None),
        P("dp"),
        P("dp"),
        P("dp"),
        P("dp", None),
        P("dp"),
        P("dp", None),
        P("dp"),
        P("dp"),
        P("dp"),
        P("dp", "seq", None),
    )
    fitted = mesh.shape["dp"] == 8 and mesh.shape["seq"] == 4
    return jax.shard_map(
        fitted_shards if fitted else general_shards,
        mesh=mesh,
        in_specs=placed,
        out_specs=(
            P("dp", "seq", None),
            P("dp", "seq", None),
            P("dp", None),
            P("dp"),
            P("dp", None),
            P("dp", None),
            P("dp"),
            P("dp", None),
            P("dp"),
            P("dp"),
            P("dp"),
            P("dp", None),
            P("dp"),
            P("dp", None),
            P("dp"),
            P("dp"),
            P("dp"),
        ),
        check_vma=False,
    )
```
